128 devices in a mesh: seq: 64 (over z, y_hi, x, core), branch: 2 (over y_lo).
Axes of the slice: x: 4, y: 4 (y_hi: 2, y_lo: 2; y = y_hi * 2 + y_lo), z: 4, core: 2. Of those that a mesh axis runs over, the one named last changes fastest.
Arguments:
- queries: bfloat16 [2, 3584, 2560], P('branch', 'seq'), may hold values from -100 to 100
- keys_values: bfloat16 [2, 3584, 2560], P(None, 'seq', 'branch'), may hold values from -10 to 10
- residual_in: bfloat16 [2, 3584, 2560], P('branch', 'seq'), may hold values from -90 to 90
- cross_gain: bfloat16 [2560], replicated, may hold values from 0.099609375 to 1.8984375
- text_kv: bfloat16 [2, 2, 512, 2560], replicated, may hold values from -90 to 90
- prompt_ids: int32 [2, 512], replicated, may hold values from 0 to 256383
- word_align: int32 [512], replicated, may hold values from 0 to 511, as said below
Outputs:
- attended: bfloat16 [2, 3584, 2560], P('branch', 'seq')
- result: bfloat16 [2, 3584, 2560], P('branch', 'seq')
The draws below stay inside these ranges and needn't reach their ends.
Inputs may be any that keep to these rules, and one draw needn't show every extreme that they name: `word_align`: a permutation of the 512 source positions.
All inputs are finite; a program needn't handle non-finite values.
Results may differ from the reference program's by a relative error of at most 0.019.
Values may be sent and summed in bfloat16 or wider, within the bound.
No kernel may reach another device: no remote copies, remote signals or barrier semaphores. Data moves between devices by JAX's collectives and lax.ppermute only.
A program may use at most 128 MiB of HBM per device.

```python
import math
import jax
import jax.numpy as jnp
from jax import lax

H = 20
HD = 128
TXT = 512
VOCAB = 256384
W = 2560
TOKENS = 3584


def attention_draw(key):
    parts = jax.random.split(jax.random.fold_in(key, 11), 3)
    width = H * HD
    key_rows = jnp.clip(jax.random.normal(parts[0], (TOKENS, width), jnp.float32), -5.0, 5.0)
    value_rows = jnp.clip(2.0 * jax.random.normal(parts[1], (TOKENS, width), jnp.float32), -10.0, 10.0)
    query_rows = jnp.clip(2.0 * jax.random.normal(parts[2], (2, TOKENS, width), jnp.float32), -8.0, 8.0)
    return (query_rows, jnp.stack([key_rows, value_rows]))


def draw_queries(key, part):
    return attention_draw(key)[0].astype(jnp.bfloat16)


def draw_keys_values(key, part):
    return attention_draw(key)[1].astype(jnp.bfloat16)


def text_draw(key):
    parts = jax.random.split(jax.random.fold_in(key, 23), 4)
    width = H * HD
    residual = jnp.clip(0.3 * jax.random.normal(parts[1], (2, TOKENS, width), jnp.float32), -2.0, 2.0)
    text_keys = jnp.clip(2.0 * jax.random.normal(parts[2], (2, TXT, width), jnp.float32), -10.0, 10.0)
    text_values = jnp.clip(4.0 * jax.random.normal(parts[3], (2, TXT, width), jnp.float32), -24.0, 24.0)
    return (residual, jnp.stack([text_keys, text_values]))


def draw_residual_in(key, part):
    return text_draw(key)[0].astype(jnp.bfloat16)


def draw_text_kv(key, part):
    return text_draw(key)[1].astype(jnp.bfloat16)


def prompt_draw(key):
    parts = jax.random.split(jax.random.fold_in(key, 37), 4)
    source_ids = jax.random.randint(parts[0], (TXT,), 0, VOCAB, dtype=jnp.int32)
    source_ids = source_ids.at[0].set(VOCAB - 1).at[1].set(0)
    position = jnp.arange(TXT, dtype=jnp.int32)
    order_score = 8 * position + jax.random.randint(parts[1], (TXT,), 0, 24, dtype=jnp.int32)
    order_score = order_score * TXT + position
    word_order = jnp.argsort(order_score).astype(jnp.int32)
    fresh_ids = jax.random.randint(parts[2], (TXT,), 0, VOCAB, dtype=jnp.int32)
    replaced = jax.random.randint(parts[3], (TXT,), 0, 4, dtype=jnp.int32) == 0
    edit_ids = jnp.where(replaced, fresh_ids, source_ids[word_order])
    return (jnp.stack([source_ids, edit_ids]).astype(jnp.int32), word_order)


def draw_prompt_ids(key, part):
    return prompt_draw(key)[0]


def draw_word_align(key, part):
    return prompt_draw(key)[1]


def setup_inputs(seed: int = 0) -> dict:
    seeds = jax.random.split(jax.random.key(seed), 8)
    queries = draw_queries(jax.random.fold_in(seeds[7], 71), 0)
    keys_values = draw_keys_values(jax.random.fold_in(seeds[7], 71), 0)
    residual_in = draw_residual_in(jax.random.fold_in(seeds[7], 71), 0)
    cross_gain = jnp.clip(1.0 + 0.18 * jax.random.normal(seeds[3], (W,), jnp.float32), 0.099609375, 1.8984375).astype(jnp.bfloat16)
    text_kv = draw_text_kv(jax.random.fold_in(seeds[7], 71), 0)
    prompt_ids = draw_prompt_ids(jax.random.fold_in(seeds[7], 71), 0)
    word_align = draw_word_align(jax.random.fold_in(seeds[7], 71), 0)
    return {"queries": queries, "keys_values": keys_values, "residual_in": residual_in, "cross_gain": cross_gain, "text_kv": text_kv, "prompt_ids": prompt_ids, "word_align": word_align}


def softmax_parts(scores):
    row_peak = lax.optimization_barrier(jnp.max(scores, axis=-1, keepdims=True))
    weights = jnp.exp(scores - row_peak)
    return (weights, lax.optimization_barrier(jnp.sum(weights, axis=-1, keepdims=True)))

def alignment(prompt_ids, word_align):
    word_pairs = jnp.arange(TXT, dtype=jnp.int32)[:, None] == word_align[None, :]
    aligned_ids = lax.optimization_barrier(jnp.sum(jnp.where(word_pairs, prompt_ids[0][:, None], 0), axis=0))
    same_word = prompt_ids[1] == aligned_ids
    selection = jnp.where(word_pairs & same_word[None, :], 1.0, 0.0).astype(jnp.float32)
    keep_own = jnp.where(same_word, 0.0, 1.0).astype(jnp.float32)
    return (selection, keep_own)

def self_attention(queries, keys_values):
    score_scale = 1.0 / math.sqrt(HD)
    query_heads = queries.reshape(2 * TOKENS, H, HD).transpose(1, 0, 2)
    key_heads = keys_values[0].reshape(TOKENS, H, HD).transpose(1, 0, 2)
    value_heads = keys_values[1].reshape(TOKENS, H, HD).transpose(1, 0, 2)

    def one_head(operands):
        query_rows, key_rows, value_rows = operands
        scores = jnp.dot(query_rows, key_rows.T, preferred_element_type=jnp.float32) * score_scale
        weights, weight_sum = softmax_parts(scores)
        summed = jnp.dot(weights.astype(jnp.bfloat16), value_rows, preferred_element_type=jnp.float32)
        return summed / weight_sum
    output = lax.map(one_head, (query_heads, key_heads, value_heads))
    return output.transpose(1, 0, 2).reshape(2, TOKENS, H * HD).astype(jnp.bfloat16)

def text_maps(cross_query, text_keys):
    query_heads = cross_query.astype(jnp.float32).reshape(TOKENS, H, HD)
    key_heads = text_keys.astype(jnp.float32).reshape(TXT, H, HD)
    scores = jnp.einsum('qhd,thd->hqt', query_heads, key_heads) * (1.0 / math.sqrt(HD))
    weights, weight_sum = softmax_parts(scores)
    return weights / weight_sum

def reference(queries, keys_values, residual_in, cross_gain, text_kv, prompt_ids, word_align):
    attended = self_attention(queries, keys_values)
    middle = residual_in.astype(jnp.float32) + attended.astype(jnp.float32)
    cross_query = (middle * lax.rsqrt(lax.optimization_barrier(jnp.mean(middle * middle, axis=-1, keepdims=True)) + 1e-06) * cross_gain.astype(jnp.float32)).astype(jnp.bfloat16)
    selection, keep_own = alignment(prompt_ids, word_align)
    source_maps = text_maps(cross_query[0], text_kv[0, 0]).astype(jnp.bfloat16)
    edit_maps = text_maps(cross_query[1], text_kv[0, 1])
    picked = jnp.einsum('hqs,sj->hqj', source_maps.astype(jnp.float32), selection)
    injected = (picked + edit_maps * keep_own).astype(jnp.bfloat16)
    outputs = []
    for branch, map_set in ((0, source_maps), (1, injected)):
        value_rows = text_kv[1, branch].astype(jnp.float32).reshape(TXT, H, HD)
        outputs.append(jnp.einsum('hqt,thd->qhd', map_set.astype(jnp.float32), value_rows).reshape(TOKENS, H * HD))
    result = (middle + jnp.stack(outputs)).astype(jnp.bfloat16)
    return (attended, result)
```

```python
import functools
import math

import jax
import jax.numpy as jnp
from jax import lax
from jax.experimental import pallas as pl
from jax.experimental.pallas import tpu as pltpu
from jax.sharding import Mesh, PartitionSpec as P

HD = 128
NQ = 5
TOK = 56
ROWS = 4 * TOK
KEYS = 2 * TOK
TXT = 512
CHUNKS = ((0, 5),)
SCALE = 1.0 / math.sqrt(HD)
LOG2E = 1.4426950408889634
PLANE = ("yh", "yl")
BF = jnp.bfloat16
F32 = jnp.float32


def shift(value, axis, distance, size):
    return lax.ppermute(value, axis, [(i, (i + distance) % size) for i in range(size)])


def dot_t(left, right):
    return lax.dot_general(left, right, (((1,), (1,)), ((), ())), preferred_element_type=F32)


def first_head(plane):
    return 10 * (plane % 2) + 5 * (plane // 2)


def vmem(count):
    return [pl.BlockSpec(memory_space=pltpu.VMEM) for _ in range(count)]


def call(kernel, out_shapes, scalars, operands, scratch=(), flops=0, exps=0, name=None):
    in_specs = [pl.BlockSpec(memory_space=pltpu.SMEM)] * len(scalars) + vmem(len(operands))
    moved = sum(math.prod(o.shape) * o.dtype.itemsize for o in operands)
    moved += sum(math.prod(o.shape) * o.dtype.itemsize for o in out_shapes)
    return pl.pallas_call(
        kernel,
        out_shape=out_shapes,
        in_specs=in_specs,
        out_specs=vmem(len(out_shapes)),
        scratch_shapes=list(scratch),
        cost_estimate=pl.CostEstimate(flops=flops, bytes_accessed=moved, transcendentals=exps),
        compiler_params=pltpu.CompilerParams(vmem_limit_bytes=40 << 20),
        name=name,
    )(*scalars, *operands)


def shaped(shape, dtype=BF):
    return jax.ShapeDtypeStruct(shape, dtype)


def split_kv_kernel(plane_ref, kv_ref, *outs):
    high = plane_ref[0] // 2
    for target, half in ((0, high), (1, 1 - high)):
        for index, (low, top) in enumerate(CHUNKS):
            out = outs[target * len(CHUNKS) + index]
            for head in range(low, top):
                lane = pl.multiple_of((half * NQ + head) * HD, HD)
                for which in range(2):
                    out[head - low, which] = kv_ref[which, :, pl.ds(lane, HD)]


def split_rows_kernel(plane_ref, rows_ref, *outs):
    for distance in range(4):
        plane = lax.rem(plane_ref[0] + distance, 4)
        for index, (low, top) in enumerate(CHUNKS):
            out = outs[distance * len(CHUNKS) + index]
            for head in range(low, top):
                lane = pl.multiple_of((first_head(plane) + head) * HD, HD)
                out[head - low] = rows_ref[:, pl.ds(lane, HD)]


def join_rows_kernel(plane_ref, *refs):
    pieces, out = refs[:-1], refs[-1]
    for distance in range(4):
        plane = lax.rem(plane_ref[0] + distance, 4)
        for index, (low, top) in enumerate(CHUNKS):
            piece = pieces[distance * len(CHUNKS) + index]
            for head in range(low, top):
                lane = pl.multiple_of((first_head(plane) + head) * HD, HD)
                out[:, pl.ds(lane, HD)] = piece[head - low]


def attend_kernel(count, *refs):
    queries, pieces = refs[:4], refs[4:12]
    outs, (keys, values, stats) = refs[12:16], refs[16:]
    lanes = lax.broadcasted_iota(jnp.int32, (ROWS, HD), 1)
    stats[...] = jnp.zeros_like(stats)

    def one_head(head, _):
        for index, piece in enumerate(pieces):
            keys[pl.ds(index * KEYS, KEYS), :] = piece[head, 0]
            values[pl.ds(index * KEYS, KEYS), :] = piece[head, 1]
        for index in range(4):
            scores = dot_t(queries[index][head], keys[...])
            peak = jnp.max(scores, axis=1, keepdims=True)
            weights = jnp.exp2(scores * (SCALE * LOG2E) - peak * (SCALE * LOG2E))
            total = jnp.sum(weights, axis=1, keepdims=True)
            summed = jnp.dot(weights.astype(BF), values[...], preferred_element_type=F32)
            outs[index][head] = (summed / total).astype(BF)
            level = peak * SCALE + jnp.log(total)
            coarse = level.astype(BF).astype(F32)
            middle = (level - coarse).astype(BF).astype(F32)
            fine = level - coarse - middle
            old = stats[index]
            old = jnp.where(lanes == head, coarse, old)
            old = jnp.where(lanes == head + 32, middle, old)
            stats[index] = jnp.where(lanes == head + 64, fine, old)
        return 0

    lax.fori_loop(0, count, one_head, 0)
    for index in range(4):
        outs[index][count] = stats[index].astype(BF)


def combine_kernel(*refs):
    count = len(CHUNKS)
    partials = [refs[4 * k : 4 * k + 4] for k in range(count)]
    residuals = [refs[4 * count + 4 * k : 4 * count + 4 * k + 4] for k in range(count)]
    outs = refs[8 * count :]
    attended = [outs[4 * k : 4 * k + 4] for k in range(count)]
    middle_ref, square_ref = outs[4 * count], outs[4 * count + 1]
    squares = jnp.zeros((ROWS, HD), F32)
    for index, (low, top) in enumerate(CHUNKS):
        size = top - low
        levels = []
        for partial in partials[index]:
            stat = partial[size].astype(F32)
            levels.append(stat + pltpu.roll(stat, HD - 32, 1) + pltpu.roll(stat, HD - 64, 1))
        peak = functools.reduce(jnp.maximum, levels)
        shares = [jnp.exp(level - peak) for level in levels]
        inverse = 1.0 / sum(shares)
        shares = [share * inverse for share in shares]
        for head in range(size):
            total = sum(
                partial[head].astype(F32) * share[:, head : head + 1]
                for partial, share in zip(partials[index], shares)
            )
            for block in range(4):
                part = total[block * TOK : (block + 1) * TOK].astype(BF)
                attended[index][block][head] = part
                middle = residuals[index][block][head].astype(F32) + part.astype(F32)
                middle_ref[low + head, block] = middle
            rows = jnp.concatenate([middle_ref[low + head, b] for b in range(4)], axis=0)
            squares = squares + rows * rows
    sums = jnp.sum(squares, axis=1, keepdims=True)
    lanes = lax.broadcasted_iota(jnp.int32, (TOK, HD), 1)
    packed = jnp.zeros((TOK, HD), F32)
    for block in range(4):
        packed = jnp.where(lanes == block, sums[block * TOK : (block + 1) * TOK], packed)
    square_ref[...] = packed


def prompt_kernel(plane_ref, ids_ref, old_ids_ref, align_ref, values_ref, mixed_ref, own_ref):
    align = align_ref[0:1, :]
    pairs = lax.broadcasted_iota(jnp.int32, (TXT, TXT), 0) == align
    aligned = jnp.sum(jnp.where(pairs, old_ids_ref[...], 0), axis=0, keepdims=True)
    same = ids_ref[1:2, :] == aligned
    own_ref[...] = jnp.broadcast_to(jnp.where(same, 0.0, 1.0), (8, TXT)).astype(F32)
    selection = jnp.where(pairs & same, 1.0, 0.0).astype(BF)
    mixed_ref[...] = jnp.dot(selection, values_ref[0, 0], preferred_element_type=F32).astype(BF)


def prompts(quarter, prompt_ids, word_align, text_kv):
    whole = lambda shape: pl.BlockSpec(shape, lambda i, q: (0,) * len(shape))
    return pl.pallas_call(
        prompt_kernel,
        out_shape=(shaped((TXT, NQ * HD)), shaped((8, TXT), F32)),
        grid_spec=pltpu.PrefetchScalarGridSpec(
            num_scalar_prefetch=1,
            grid=(1,),
            in_specs=[
                whole((2, TXT)),
                whole((TXT, 1)),
                whole((1, TXT)),
                pl.BlockSpec((1, 1, TXT, NQ * HD), lambda i, q: (1, 1, 0, q[0])),
            ],
            out_specs=(whole((TXT, NQ * HD)), whole((8, TXT))),
        ),
        cost_estimate=pl.CostEstimate(
            flops=2 * TXT * TXT * NQ * HD, bytes_accessed=2 << 20, transcendentals=0
        ),
        name="prompts",
    )(quarter, prompt_ids, prompt_ids[0].reshape(TXT, 1), word_align.reshape(1, TXT), text_kv)


def softmax(scores):
    peak = jnp.max(scores, axis=1, keepdims=True)
    weights = jnp.exp2(scores * (SCALE * LOG2E) - peak * (SCALE * LOG2E))
    return weights * (1.0 / jnp.sum(weights, axis=1, keepdims=True))


def cross_kernel(info_ref, middle_ref, s0, s1, s2, s3, gain_ref, text_ref, mixed_ref, own_ref, *refs):
    outs, (scale_ref, done_ref) = refs[:4], refs[4:]
    odd = lax.rem(info_ref[1], 2)
    squares = s0[...]
    lanes = lax.broadcasted_iota(jnp.int32, (TOK, HD), 1)
    for distance, ref in ((1, s1), (2, s2), (3, s3)):
        other = ref[...]
        turned = pltpu.roll(other, distance, 1)
        wrapped = pltpu.roll(other, HD - 4 + distance, 1)
        squares = squares + jnp.where(lanes < distance, wrapped, turned)
    norm = lax.rsqrt(squares * (1.0 / (4 * NQ * HD)) + 1e-06)
    for block in range(4):
        scale_ref[block] = jnp.broadcast_to(norm[:, block : block + 1], (TOK, HD))
    pairs = ((odd, 3 * (1 - odd)), (2 + odd, 1 + odd))
    own = own_ref[0:1, :]
    for head in range(NQ):
        columns = slice(head * HD, (head + 1) * HD)
        gain = gain_ref[0:1, columns].astype(F32)
        middles, asked = [], []
        for side in range(2):
            rows = jnp.concatenate([middle_ref[head, pair[side]] for pair in pairs], axis=0)
            norms = jnp.concatenate([scale_ref[pair[side]] for pair in pairs], axis=0)
            middles.append(rows)
            asked.append((rows * norms * gain).astype(BF))
        source = softmax(dot_t(asked[0], text_ref[0, 0, :, columns])).astype(BF)
        edited = (softmax(dot_t(asked[1], text_ref[0, 1, :, columns])) * own).astype(BF)
        results = (
            jnp.dot(source, text_ref[1, 0, :, columns], preferred_element_type=F32),
            jnp.dot(source, mixed_ref[:, columns], preferred_element_type=F32)
            + jnp.dot(edited, text_ref[1, 1, :, columns], preferred_element_type=F32),
        )
        for side in range(2):
            rows = middles[side] + results[side]
            for index, pair in enumerate(pairs):
                done_ref[pair[side]] = rows[index * TOK : (index + 1) * TOK]
        for block in range(4):
            outs[block][head] = done_ref[block].astype(BF)


def cross(info, middle, squares, gain, text_kv, mixed, own):
    whole = lambda shape: pl.BlockSpec(shape, lambda i, q: (0,) * len(shape))
    piece = (NQ, TOK, HD)
    return pl.pallas_call(
        cross_kernel,
        out_shape=(shaped(piece),) * 4,
        grid_spec=pltpu.PrefetchScalarGridSpec(
            num_scalar_prefetch=1,
            grid=(1,),
            in_specs=[
                whole((NQ, 4, TOK, HD)),
                *[whole((TOK, HD))] * 4,
                pl.BlockSpec((1, NQ * HD), lambda i, q: (0, q[0])),
                pl.BlockSpec((2, 2, TXT, NQ * HD), lambda i, q: (0, 0, 0, q[0])),
                whole((TXT, NQ * HD)),
                whole((8, TXT)),
            ],
            out_specs=(whole(piece),) * 4,
            scratch_shapes=[pltpu.VMEM((4, TOK, HD), F32), pltpu.VMEM((4, TOK, HD), F32)],
        ),
        compiler_params=pltpu.CompilerParams(vmem_limit_bytes=40 << 20),
        cost_estimate=pl.CostEstimate(
            flops=2 * 5 * 112 * TXT * NQ * HD, bytes_accessed=5 << 20, transcendentals=224 * NQ * TXT
        ),
        name="cross",
    )(info, middle, *squares, gain, text_kv, mixed, own)


def per_device(queries, keys_values, residual_in, cross_gain, text_kv, prompt_ids, word_align):
    plane = 2 * lax.axis_index("yh") + lax.axis_index("yl")
    quarter = 2 * lax.axis_index("yl") + lax.axis_index("yh")
    where = plane.reshape(1).astype(jnp.int32)
    sizes = [top - low for low, top in CHUNKS]
    count = len(CHUNKS)

    def split_rows(rows, name):
        shapes = [shaped((n, TOK, HD)) for n in sizes] * 4
        flat = call(split_rows_kernel, shapes, [where], [rows], name=name)
        pieces = [flat[d * count : (d + 1) * count] for d in range(4)]
        return [
            [p if d == 0 else shift(p, PLANE, d, 4) for p in pieces[d]] for d in range(4)
        ]

    kv_shapes = [shaped((n, 2, TOK, HD)) for n in sizes] * 2
    kv_flat = call(split_kv_kernel, kv_shapes, [where], [keys_values], name="split_kv")
    query_blocks = split_rows(queries[0], "split_queries")
    partials = []
    for k in range(count):
        n = sizes[k]
        near = jnp.concatenate([kv_flat[k], shift(kv_flat[count + k], PLANE, 2, 4)], axis=2)
        mine = jnp.concatenate([query_blocks[d][k] for d in range(4)], axis=1)
        along = [near] + [shift(near, "z", d, 4) for d in (1, 3, 2)]
        across = [shift(piece, "c", 1, 2) for piece in along]
        rows = [mine] + [shift(mine, "x", d, 4) for d in (1, 3, 2)]
        outs = call(
            functools.partial(attend_kernel, n),
            [shaped((n + 1, ROWS, HD))] * 4,
            [],
            [*rows, *along, *across],
            scratch=[
                pltpu.VMEM((8 * KEYS, HD), BF),
                pltpu.VMEM((8 * KEYS, HD), BF),
                pltpu.VMEM((4, ROWS, HD), F32),
            ],
            flops=4 * n * 4 * ROWS * 8 * KEYS * HD,
            exps=n * 4 * ROWS * 8 * KEYS,
            name="attend",
        )
        partials.append(
            [outs[0]] + [shift(outs[i], "x", -d, 4) for i, d in ((1, 1), (2, 3), (3, 2))]
        )
    residual_blocks = split_rows(residual_in[0], "split_residual")
    mixed, own = prompts(quarter.reshape(1).astype(jnp.int32), prompt_ids, word_align, text_kv)
    out_shapes = [shaped((n, TOK, HD)) for n in sizes for _ in range(4)]
    out_shapes += [shaped((NQ, 4, TOK, HD), F32), shaped((TOK, HD), F32)]
    combined = call(
        combine_kernel,
        out_shapes,
        [],
        [p for part in partials for p in part]
        + [residual_blocks[d][k] for k in range(count) for d in range(4)],
        name="combine",
    )
    middle, square = combined[4 * count], combined[4 * count + 1]
    squares = [square] + [shift(square, PLANE, d, 4) for d in (1, 2, 3)]
    info = jnp.stack([quarter, plane]).astype(jnp.int32)
    results = cross(info, middle, squares, cross_gain.reshape(1, -1), text_kv, mixed, own)

    def join(pieces, name):
        home = [[p if d == 0 else shift(p, PLANE, -d, 4) for p in pieces[d]] for d in range(4)]
        return call(
            join_rows_kernel,
            [shaped((TOK, 4 * NQ * HD))],
            [where],
            [p for d in range(4) for p in home[d]],
            name=name,
        )[0]

    attended = join([[combined[4 * k + d] for k in range(count)] for d in range(4)], "join_attended")
    pieces = [[results[d][low:top] for low, top in CHUNKS] for d in range(4)]
    result = join(pieces, "join_result")
    return (attended[None], result[None])


def solution(mesh):
    grid = Mesh(mesh.devices.reshape(4, 2, 4, 2, 2), ("z", "yh", "x", "c", "yl"))
    seq = ("z", "yh", "x", "c")
    in_specs = (
        P("yl", seq, None),
        P(None, seq, "yl"),
        P("yl", seq, None),
        P(),
        P(),
        P(),
        P(),
    )
    out_specs = (P("yl", seq, None), P("yl", seq, None))
    return jax.shard_map(
        per_device, mesh=grid, in_specs=in_specs, out_specs=out_specs, check_vma=False
    )
```

```python
import functools
import math

import jax
import jax.numpy as jnp
from jax import lax
from jax.experimental import pallas as pl
from jax.experimental.pallas import tpu as pltpu
from jax.sharding import Mesh, PartitionSpec as P

HD = 128
NQ = 5
TOK = 56
ROWS = 4 * TOK
KEYS = 2 * TOK
TXT = 512
GROUPS = ((0, 3, "x", "z"), (3, 2, "z", "x"))
STAT = 32
SCALE = 1.0 / math.sqrt(HD)
LOG2E = 1.4426950408889634
PLANE = ("yh", "yl")
BF = jnp.bfloat16
F32 = jnp.float32


def shift(value, axis, distance, size):
    return lax.ppermute(value, axis, [(i, (i + distance) % size) for i in range(size)])


def dot_t(left, right):
    return lax.dot_general(left, right, (((1,), (1,)), ((), ())), preferred_element_type=F32)


def first_head(plane):
    return 10 * (plane % 2) + 5 * (plane // 2)


def vmem(count):
    return [pl.BlockSpec(memory_space=pltpu.VMEM) for _ in range(count)]


def call(kernel, out_shapes, scalars, operands, scratch=(), flops=0, exps=0, name=None):
    in_specs = [pl.BlockSpec(memory_space=pltpu.SMEM)] * len(scalars) + vmem(len(operands))
    moved = sum(math.prod(o.shape) * o.dtype.itemsize for o in operands)
    moved += sum(math.prod(o.shape) * o.dtype.itemsize for o in out_shapes)
    return pl.pallas_call(
        kernel,
        out_shape=out_shapes,
        in_specs=in_specs,
        out_specs=vmem(len(out_shapes)),
        scratch_shapes=list(scratch),
        cost_estimate=pl.CostEstimate(flops=flops, bytes_accessed=moved, transcendentals=exps),
        compiler_params=pltpu.CompilerParams(vmem_limit_bytes=40 << 20),
        name=name,
    )(*scalars, *operands)


def shaped(shape, dtype=BF):
    return jax.ShapeDtypeStruct(shape, dtype)


def stacked(parts):
    return jnp.concatenate([part.astype(F32) for part in parts], axis=0).astype(BF)


def split_kernel(plane_ref, rows_ref, kv_ref, kept, first, last, across, own):
    high = plane_ref[0] // 2
    outs = (own, first, across, last)
    for distance in range(4):
        plane = lax.rem(plane_ref[0] + distance, 4)
        for head in range(NQ):
            lane = pl.multiple_of((first_head(plane) + head) * HD, HD)
            outs[distance][head] = rows_ref[:, pl.ds(lane, HD)]
    for head in range(NQ):
        here = pl.multiple_of((high * NQ + head) * HD, HD)
        there = pl.multiple_of(((1 - high) * NQ + head) * HD, HD)
        for which in range(2):
            kept[2 * head + which] = kv_ref[which, :, pl.ds(here, HD)]
            across[NQ + 2 * head + which] = kv_ref[which, :, pl.ds(there, HD)]


def pack_kernel(kept, own, first, across, last, along_x, along_z, swap):
    queries = (own, first, across, last)
    for group, (low, count, _, _) in enumerate(GROUPS):
        to_rows, to_keys = (along_x, along_z) if group == 0 else (along_z, along_x)
        start_rows = 0 if group == 0 else low * ROWS
        start_keys = 0 if group == 0 else low * ROWS
        for index in range(count):
            head = low + index
            to_rows[start_rows + index * ROWS : start_rows + (index + 1) * ROWS, :] = stacked(
                [query[head] for query in queries]
            )
            keys = stacked(
                [kept[2 * head], across[NQ + 2 * head], kept[2 * head + 1], across[NQ + 2 * head + 1]]
            )
            to_keys[start_keys + index * ROWS : start_keys + (index + 1) * ROWS, :] = keys
            swap[head * ROWS : (head + 1) * ROWS, :] = keys


BASES = ((0, 0), (GROUPS[0][1] * ROWS, GROUPS[0][1] * ROWS))


def repack_kernel(*refs):
    from_x, from_z, out = refs[:3], refs[3:6], refs[7]
    wide, narrow = (count * ROWS for _, count, _, _ in GROUPS)
    for index in range(3):
        out[index * wide : (index + 1) * wide, :] = from_z[index][0:wide, :]
        start = 3 * wide + index * narrow
        out[start : start + narrow, :] = from_x[index][wide : wide + narrow, :]


def join_rows_kernel(plane_ref, *refs):
    pieces, out = refs[:-1], refs[-1]
    for distance in range(4):
        plane = lax.rem(plane_ref[0] + distance, 4)
        for head in range(NQ):
            lane = pl.multiple_of((first_head(plane) + head) * HD, HD)
            out[:, pl.ds(lane, HD)] = pieces[distance][head]


def attend_kernel(group, *refs):
    _, count, _, _ = GROUPS[group]
    from_x, from_z, swapped, others = refs[:4], refs[4:8], refs[8], refs[9]
    rows_of, keys_of = (from_x, from_z) if group == 0 else (from_z, from_x)
    row_base, key_base = BASES[group]
    wide = GROUPS[0][1] * ROWS
    size = count * ROWS
    other_base = 0 if group == 0 else 3 * wide
    pieces = [(ref, key_base) for ref in keys_of] + [(swapped, key_base)]
    pieces += [(others, other_base + index * size) for index in range(3)]
    refs = refs[11:]
    outs, (keys, values, stats) = refs[:4], refs[-3:]
    lanes = lax.broadcasted_iota(jnp.int32, (ROWS, HD), 1)
    stats[...] = jnp.zeros_like(stats)

    def one_head(head, _):
        for index, (piece, base) in enumerate(pieces):
            start = pl.multiple_of(base + head * ROWS, 16)
            keys[pl.ds(index * KEYS, KEYS), :] = piece[pl.ds(start, KEYS), :]
            values[pl.ds(index * KEYS, KEYS), :] = piece[
                pl.ds(pl.multiple_of(start + KEYS, 16), KEYS), :
            ]
        for index in range(4):
            start = pl.multiple_of(row_base + head * ROWS, 16)
            scores = dot_t(rows_of[index][pl.ds(start, ROWS), :], keys[...])
            peak = jnp.max(scores, axis=1, keepdims=True)
            weights = jnp.exp2(scores * (SCALE * LOG2E) - peak * (SCALE * LOG2E))
            total = jnp.sum(weights, axis=1, keepdims=True)
            summed = jnp.dot(weights.astype(BF), values[...], preferred_element_type=F32)
            outs[index][pl.ds(pl.multiple_of(head * ROWS, 16), ROWS), :] = (summed / total).astype(BF)
            level = peak * SCALE + jnp.log(total)
            coarse = level.astype(BF).astype(F32)
            middle = (level - coarse).astype(BF).astype(F32)
            fine = level - coarse - middle
            old = stats[index, 0:ROWS, :]
            old = jnp.where(lanes == 3 * head, coarse, old)
            old = jnp.where(lanes == 3 * head + 1, middle, old)
            stats[index, 0:ROWS, :] = jnp.where(lanes == 3 * head + 2, fine, old)
        return 0

    lax.fori_loop(0, count, one_head, 0)
    for index in range(4):
        turned = stats[index].T
        outs[index][size : size + 16, :] = turned[0:16, 0:HD].astype(BF)
        outs[index][size + 16 : size + STAT, :] = turned[0:16, HD : 2 * HD].astype(BF)


def attend(group, from_x, from_z, swapped, others, after):
    _, count, _, _ = GROUPS[group]
    return call(
        functools.partial(attend_kernel, group),
        [shaped((count * ROWS + STAT, HD))] * 4,
        [],
        [*from_x, *from_z, swapped, others, after],
        scratch=[
            pltpu.VMEM((8 * KEYS, HD), BF),
            pltpu.VMEM((8 * KEYS, HD), BF),
            pltpu.VMEM((4, 2 * HD, HD), F32),
        ],
        flops=4 * count * 4 * ROWS * 8 * KEYS * HD,
        exps=count * 4 * ROWS * 8 * KEYS,
        name="attend_rows_x" if group == 0 else "attend_rows_z",
    )


def split_rows_kernel(plane_ref, rows_ref, after_ref, *outs):
    for distance in range(4):
        plane = lax.rem(plane_ref[0] + distance, 4)
        for head in range(NQ):
            lane = pl.multiple_of((first_head(plane) + head) * HD, HD)
            outs[distance][head] = rows_ref[:, pl.ds(lane, HD)]


def combine_kernel(*refs):
    partials = (refs[:4], refs[4:8])
    residuals, attended = refs[8:12], refs[12:16]
    middle_ref, turn_ref = refs[16:]
    turn_ref[...] = jnp.zeros_like(turn_ref)
    squares = jnp.zeros((ROWS, HD), F32)
    for group, (low, count, _, _) in enumerate(GROUPS):
        size = count * ROWS
        levels = []
        for partial in partials[group]:
            turn_ref[0:16, 0:HD] = partial[size : size + 16, :].astype(F32)
            turn_ref[0:16, HD : 2 * HD] = partial[size + 16 : size + STAT, :].astype(F32)
            stat = turn_ref[...].T[0:ROWS, :]
            levels.append(stat + pltpu.roll(stat, HD - 1, 1) + pltpu.roll(stat, HD - 2, 1))
        peak = functools.reduce(jnp.maximum, levels)
        shares = [jnp.exp(level - peak) for level in levels]
        inverse = 1.0 / sum(shares)
        shares = [share * inverse for share in shares]
        for index in range(count):
            head = low + index
            total = sum(
                partial[index * ROWS : (index + 1) * ROWS, :].astype(F32)
                * share[:, 3 * index : 3 * index + 1]
                for partial, share in zip(partials[group], shares)
            )
            middles = []
            for block in range(4):
                part = total[block * TOK : (block + 1) * TOK].astype(BF)
                attended[block][head] = part
                middle = residuals[block][head].astype(F32) + part.astype(F32)
                middle_ref[head, block] = middle
                middles.append(middle)
            rows = jnp.concatenate(middles, axis=0)
            squares = squares + rows * rows
    sums = jnp.sum(squares, axis=1, keepdims=True)
    lanes = lax.broadcasted_iota(jnp.int32, (TOK, HD), 1)
    packed = jnp.zeros((TOK, HD), F32)
    for block in range(4):
        column = sums[block * TOK : (block + 1) * TOK]
        coarse = column.astype(BF).astype(F32)
        middle = (column - coarse).astype(BF).astype(F32)
        packed = jnp.where(lanes == block, coarse, packed)
        packed = jnp.where(lanes == block + 32, middle, packed)
        packed = jnp.where(lanes == block + 64, column - coarse - middle, packed)
    for block in range(4):
        attended[block][NQ] = packed.astype(BF)


def prompt_kernel(
    plane_ref, ids_ref, old_ids_ref, align_ref, gain_ref, text_ref, mixed_ref, own_ref, copy_ref, scale_ref
):
    align = align_ref[0:1, :]
    pairs = lax.broadcasted_iota(jnp.int32, (TXT, TXT), 0) == align
    aligned = jnp.sum(jnp.where(pairs, old_ids_ref[...], 0), axis=0, keepdims=True)
    same = ids_ref[1:2, :] == aligned
    own_ref[...] = jnp.broadcast_to(jnp.where(same, 0.0, 1.0), (8, TXT)).astype(F32)
    selection = jnp.where(pairs & same, 1.0, 0.0).astype(BF)
    mixed_ref[...] = jnp.dot(selection, text_ref[1, 1], preferred_element_type=F32).astype(BF)
    copy_ref[...] = text_ref[...]
    scale_ref[...] = jnp.broadcast_to(gain_ref[0:1, :].astype(F32), (8, NQ * HD))


def prompts(quarter, prompt_ids, word_align, gain, text_kv):
    whole = lambda shape: pl.BlockSpec(shape, lambda i, q: (0,) * len(shape))
    return pl.pallas_call(
        prompt_kernel,
        out_shape=(shaped((TXT, NQ * HD)), shaped((8, TXT), F32), shaped((2, 2, TXT, NQ * HD)), shaped((8, NQ * HD), F32)),
        grid_spec=pltpu.PrefetchScalarGridSpec(
            num_scalar_prefetch=1,
            grid=(1,),
            in_specs=[
                whole((2, TXT)),
                whole((TXT, 1)),
                whole((1, TXT)),
                pl.BlockSpec((1, NQ * HD), lambda i, q: (0, q[0])),
                pl.BlockSpec((2, 2, TXT, NQ * HD), lambda i, q: (0, 0, 0, q[0])),
            ],
            out_specs=(
                whole((TXT, NQ * HD)),
                whole((8, TXT)),
                whole((2, 2, TXT, NQ * HD)),
                whole((8, NQ * HD)),
            ),
        ),
        compiler_params=pltpu.CompilerParams(vmem_limit_bytes=52 << 20),
        cost_estimate=pl.CostEstimate(
            flops=2 * TXT * TXT * NQ * HD, bytes_accessed=6 << 20, transcendentals=0
        ),
        name="prompts",
    )(
        quarter,
        prompt_ids,
        prompt_ids[0].reshape(TXT, 1),
        word_align.reshape(1, TXT),
        gain.reshape(1, -1),
        text_kv,
    )


def softmax(scores):
    peak = jnp.max(scores, axis=1, keepdims=True)
    weights = jnp.exp2(scores * (SCALE * LOG2E) - peak * (SCALE * LOG2E))
    return weights * (1.0 / jnp.sum(weights, axis=1, keepdims=True))


def cross_kernel(info_ref, middle_ref, s0, s1, s2, s3, gain_ref, text_ref, mixed_ref, own_ref, *refs):
    outs, (scale_ref, done_ref) = refs[:4], refs[4:]
    odd = lax.rem(info_ref[1], 2)
    lanes = lax.broadcasted_iota(jnp.int32, (TOK, HD), 1)

    def sums_of(ref):
        packed = ref[NQ].astype(F32)
        return packed + pltpu.roll(packed, HD - 32, 1) + pltpu.roll(packed, HD - 64, 1)

    squares = sums_of(s0)
    for distance, ref in ((1, s1), (2, s2), (3, s3)):
        other = sums_of(ref)
        turned = pltpu.roll(other, HD - distance, 1)
        wrapped = pltpu.roll(other, 4 - distance, 1)
        squares = squares + jnp.where(lanes < 4 - distance, turned, wrapped)
    norm = lax.rsqrt(squares * (1.0 / (4 * NQ * HD)) + 1e-06)
    for block in range(4):
        scale_ref[block] = jnp.broadcast_to(norm[:, block : block + 1], (TOK, HD))
    pairs = ((odd, 3 * (1 - odd)), (2 + odd, 1 + odd))
    own = own_ref[0:1, :]
    for head in range(NQ):
        columns = slice(head * HD, (head + 1) * HD)
        gain = gain_ref[0:1, columns]
        middles, asked = [], []
        for side in range(2):
            rows = jnp.concatenate([middle_ref[head, pair[side]] for pair in pairs], axis=0)
            norms = jnp.concatenate([scale_ref[pair[side]] for pair in pairs], axis=0)
            middles.append(rows)
            asked.append((rows * norms * gain).astype(BF))
        source = softmax(dot_t(asked[0], text_ref[0, 0, :, columns])).astype(BF)
        edited = (softmax(dot_t(asked[1], text_ref[0, 1, :, columns])) * own).astype(BF)
        results = (
            jnp.dot(source, text_ref[1, 0, :, columns], preferred_element_type=F32),
            jnp.dot(source, mixed_ref[:, columns], preferred_element_type=F32)
            + jnp.dot(edited, text_ref[1, 1, :, columns], preferred_element_type=F32),
        )
        for side in range(2):
            rows = middles[side] + results[side]
            for index, pair in enumerate(pairs):
                done_ref[pair[side]] = rows[index * TOK : (index + 1) * TOK]
        for block in range(4):
            outs[block][head] = done_ref[block].astype(BF)


def cross(info, middle, squares, gain, text, mixed, own):
    return call(
        cross_kernel,
        [shaped((NQ, TOK, HD))] * 4,
        [info],
        [middle, *squares, gain, text, mixed, own],
        scratch=[pltpu.VMEM((4, TOK, HD), F32), pltpu.VMEM((4, TOK, HD), F32)],
        flops=2 * 5 * 112 * TXT * NQ * HD,
        exps=224 * NQ * TXT,
        name="cross",
    )


def per_device(queries, keys_values, residual_in, cross_gain, text_kv, prompt_ids, word_align):
    plane = 2 * lax.axis_index("yh") + lax.axis_index("yl")
    quarter = 2 * lax.axis_index("yl") + lax.axis_index("yh")
    where = plane.reshape(1).astype(jnp.int32)
    info = jnp.stack([quarter, plane]).astype(jnp.int32)
    piece = (NQ, TOK, HD)

    kept, first, last, over, mine = call(
        split_kernel,
        [shaped((2 * NQ, TOK, HD)), shaped(piece), shaped(piece), shaped((3 * NQ, TOK, HD)), shaped(piece)],
        [where],
        [queries[0], keys_values],
        name="split",
    )
    over = shift(over, PLANE, 2, 4)
    first = shift(first, PLANE, 1, 4)
    last = shift(last, PLANE, 3, 4)
    buffer = shaped((NQ * ROWS, HD))
    along_x, along_z, swap = call(
        pack_kernel, [buffer] * 3, [], [kept, mine, first, over, last], name="pack"
    )
    swapped = shift(swap, "c", 1, 2)
    from_x = [along_x] + [shift(along_x, "x", d, 4) for d in (1, 3, 2)]
    from_z = [along_z] + [shift(along_z, "z", d, 4) for d in (1, 3, 2)]
    others = call(
        repack_kernel, [shaped((3 * NQ * ROWS, HD))], [], [*from_x[1:], *from_z[1:], swapped], name="repack"
    )[0]
    others = shift(others, "c", 1, 2)
    mixed, own, text, gain = prompts(
        quarter.reshape(1).astype(jnp.int32), prompt_ids, word_align, cross_gain, text_kv
    )
    partials = []
    for group, (_, _, row_axis, _) in enumerate(GROUPS):
        outs = attend(group, from_x, from_z, swapped, others, own)
        partials += [outs[0]] + [shift(outs[i], row_axis, -d, 4) for i, d in ((1, 1), (2, 3), (3, 2))]
    residuals = call(
        split_rows_kernel, [shaped(piece)] * 4, [where], [residual_in[0], outs[0]], name="split_residual"
    )
    residuals = [p if d == 0 else shift(p, PLANE, d, 4) for d, p in enumerate(residuals)]
    combined = call(
        combine_kernel,
        [shaped((NQ + 1, TOK, HD))] * 4 + [shaped((NQ, 4, TOK, HD), F32)],
        [],
        [*partials, *residuals],
        scratch=[pltpu.VMEM((HD, 2 * HD), F32)],
        name="combine",
    )
    middle = combined[4]

    def home(pieces):
        return [p if d == 0 else shift(p, PLANE, -d, 4) for d, p in enumerate(pieces)]

    def join(pieces, name):
        return call(join_rows_kernel, [shaped((TOK, 4 * NQ * HD))], [where], pieces, name=name)[0]

    attended = home(combined[:4])
    results = cross(info, middle, attended, gain, text, mixed, own)
    return (join(attended, "join_attended")[None], join(home(results), "join_result")[None])


def solution(mesh):
    grid = Mesh(mesh.devices.reshape(4, 2, 4, 2, 2), ("z", "yh", "x", "c", "yl"))
    seq = ("z", "yh", "x", "c")
    in_specs = (
        P("yl", seq, None),
        P(None, seq, "yl"),
        P("yl", seq, None),
        P(),
        P(),
        P(),
        P(),
    )
    out_specs = (P("yl", seq, None), P("yl", seq, None))
    return jax.shard_map(
        per_device, mesh=grid, in_specs=in_specs, out_specs=out_specs, check_vma=False
    )
```

```python
import functools
import math

import jax
import jax.numpy as jnp
from jax import lax
from jax.experimental import pallas as pl
from jax.experimental.pallas import tpu as pltpu
from jax.sharding import Mesh, PartitionSpec as P


HD = 128
NQ = 5
TOK = 56
ROWS = 4 * TOK
KEYS = 2 * TOK
TXT = 512
GROUPS = ((0, 3, "x", "z"), (3, 2, "z", "x"))
STAT = 32
SCALE = 1.0 / math.sqrt(HD)
LOG2E = 1.4426950408889634
PLANE = ("yh", "yl")
BF = jnp.bfloat16
F32 = jnp.float32


def shift(value, axis, distance, size):
    return lax.ppermute(value, axis, [(i, (i + distance) % size) for i in range(size)])


def dot_t(left, right):
    return lax.dot_general(left, right, (((1,), (1,)), ((), ())), preferred_element_type=F32)


def first_head(plane):
    return 10 * (plane % 2) + 5 * (plane // 2)


def vmem(count):
    return [pl.BlockSpec(memory_space=pltpu.VMEM) for _ in range(count)]


def call(kernel, out_shapes, scalars, operands, kept=(), scratch=(), flops=0, exps=0, limit=40):
    in_specs = [pl.BlockSpec(memory_space=pltpu.SMEM)] * len(scalars) + vmem(len(operands))
    in_specs += [pl.BlockSpec(memory_space=space) for _, space in kept]
    moved = sum(math.prod(o.shape) * o.dtype.itemsize for o in operands)
    moved += sum(math.prod(o.shape) * o.dtype.itemsize for o in out_shapes)
    return pl.pallas_call(
        kernel,
        out_shape=out_shapes,
        in_specs=in_specs,
        out_specs=vmem(len(out_shapes)),
        scratch_shapes=list(scratch),
        cost_estimate=pl.CostEstimate(flops=flops, bytes_accessed=moved, transcendentals=exps),
        compiler_params=pltpu.CompilerParams(vmem_limit_bytes=limit << 20),
    )(*scalars, *operands, *(array for array, _ in kept))


def shaped(shape, dtype=BF):
    return jax.ShapeDtypeStruct(shape, dtype)


def stacked(parts):
    return jnp.concatenate([part.astype(F32) for part in parts], axis=0).astype(BF)


def split_kernel(plane_ref, rows_ref, kv_ref, kept, first, last, across, own):
    high = plane_ref[0] // 2
    outs = (own, first, across, last)
    for distance in range(4):
        plane = lax.rem(plane_ref[0] + distance, 4)
        for head in range(NQ):
            lane = pl.multiple_of((first_head(plane) + head) * HD, HD)
            outs[distance][head] = rows_ref[:, pl.ds(lane, HD)]
    for head in range(NQ):
        here = pl.multiple_of((high * NQ + head) * HD, HD)
        there = pl.multiple_of(((1 - high) * NQ + head) * HD, HD)
        for which in range(2):
            kept[2 * head + which] = kv_ref[which, :, pl.ds(here, HD)]
            across[NQ + 2 * head + which] = kv_ref[which, :, pl.ds(there, HD)]


def split_rows_kernel(plane_ref, rows_ref, *outs):
    for distance in range(4):
        plane = lax.rem(plane_ref[0] + distance, 4)
        for head in range(NQ):
            lane = pl.multiple_of((first_head(plane) + head) * HD, HD)
            outs[distance][head] = rows_ref[:, pl.ds(lane, HD)]


def pack_kernel(kept, own, first, across, last, *outs):
    queries = (own, first, across, last)
    for group, (low, count, _, _) in enumerate(GROUPS):
        rows, keys = outs[2 * group], outs[2 * group + 1]
        for index in range(count):
            head = low + index
            rows[index * ROWS : (index + 1) * ROWS, :] = stacked([query[head] for query in queries])
            keys[index * ROWS : (index + 1) * ROWS, :] = stacked(
                [kept[2 * head], across[NQ + 2 * head], kept[2 * head + 1], across[NQ + 2 * head + 1]]
            )


def repack_kernel(*refs):
    out = refs[4]
    size = refs[0].shape[0]
    for index in range(4):
        out[index * size : (index + 1) * size, :] = refs[index][...]


def join_rows_kernel(plane_ref, *refs):
    pieces, out = refs[:-1], refs[-1]
    for distance in range(4):
        plane = lax.rem(plane_ref[0] + distance, 4)
        for head in range(NQ):
            lane = pl.multiple_of((first_head(plane) + head) * HD, HD)
            out[:, pl.ds(lane, HD)] = pieces[distance][head]


def attend_kernel(count, *refs):
    rows_of, keys_of, swapped = refs[:4], refs[4:8], refs[8]
    outs, (keys, values, stats) = refs[9:13], refs[13:]
    size = count * ROWS
    pieces = [(ref, 0) for ref in keys_of] + [(swapped, index * size) for index in range(4)]
    lanes = lax.broadcasted_iota(jnp.int32, (ROWS, HD), 1)
    stats[...] = jnp.zeros_like(stats)

    def one_head(head, _):
        for index, (piece, base) in enumerate(pieces):
            start = pl.multiple_of(base + head * ROWS, 16)
            keys[pl.ds(index * KEYS, KEYS), :] = piece[pl.ds(start, KEYS), :]
            values[pl.ds(index * KEYS, KEYS), :] = piece[
                pl.ds(pl.multiple_of(start + KEYS, 16), KEYS), :
            ]
        for index in range(4):
            start = pl.multiple_of(head * ROWS, 16)
            scores = dot_t(rows_of[index][pl.ds(start, ROWS), :], keys[...])
            peak = jnp.max(scores, axis=1, keepdims=True)
            weights = jnp.exp2(scores * (SCALE * LOG2E) - peak * (SCALE * LOG2E))
            total = jnp.sum(weights, axis=1, keepdims=True)
            summed = jnp.dot(weights.astype(BF), values[...], preferred_element_type=F32)
            outs[index][pl.ds(pl.multiple_of(head * ROWS, 16), ROWS), :] = (summed / total).astype(BF)
            level = peak * SCALE + jnp.log(total)
            coarse = level.astype(BF).astype(F32)
            middle = (level - coarse).astype(BF).astype(F32)
            fine = level - coarse - middle
            old = stats[index, 0:ROWS, :]
            old = jnp.where(lanes == 3 * head, coarse, old)
            old = jnp.where(lanes == 3 * head + 1, middle, old)
            stats[index, 0:ROWS, :] = jnp.where(lanes == 3 * head + 2, fine, old)
        return 0

    lax.fori_loop(0, count, one_head, 0)
    for index in range(4):
        turned = stats[index].T
        outs[index][size : size + 16, :] = turned[0:16, 0:HD].astype(BF)
        outs[index][size + 16 : size + STAT, :] = turned[0:16, HD : 2 * HD].astype(BF)


def attend(group, rows, keys, swapped):
    _, count, _, _ = GROUPS[group]
    return call(
        functools.partial(attend_kernel, count),
        [shaped((count * ROWS + STAT, HD))] * 4,
        [],
        [*rows, *keys, swapped],
        scratch=[
            pltpu.VMEM((8 * KEYS, HD), BF),
            pltpu.VMEM((8 * KEYS, HD), BF),
            pltpu.VMEM((4, 2 * HD, HD), F32),
        ],
        flops=4 * count * 4 * ROWS * 8 * KEYS * HD,
        exps=count * 4 * ROWS * 8 * KEYS,
    )


def combine_kernel(*refs):
    partials = (refs[:4], refs[4:8])
    residuals, attended = refs[8:12], refs[13:17]
    middle_ref, turn_ref = refs[17:]
    turn_ref[...] = jnp.zeros_like(turn_ref)
    squares = jnp.zeros((ROWS, HD), F32)
    for group, (low, count, _, _) in enumerate(GROUPS):
        size = count * ROWS
        levels = []
        for partial in partials[group]:
            turn_ref[0:16, 0:HD] = partial[size : size + 16, :].astype(F32)
            turn_ref[0:16, HD : 2 * HD] = partial[size + 16 : size + STAT, :].astype(F32)
            stat = turn_ref[...].T[0:ROWS, :]
            levels.append(stat + pltpu.roll(stat, HD - 1, 1) + pltpu.roll(stat, HD - 2, 1))
        peak = functools.reduce(jnp.maximum, levels)
        shares = [jnp.exp(level - peak) for level in levels]
        inverse = 1.0 / sum(shares)
        shares = [share * inverse for share in shares]
        for index in range(count):
            head = low + index
            total = sum(
                partial[index * ROWS : (index + 1) * ROWS, :].astype(F32)
                * share[:, 3 * index : 3 * index + 1]
                for partial, share in zip(partials[group], shares)
            )
            middles = []
            for block in range(4):
                part = total[block * TOK : (block + 1) * TOK].astype(BF)
                attended[block][head] = part
                middle = residuals[block][head].astype(F32) + part.astype(F32)
                middle_ref[head, block] = middle
                middles.append(middle)
            rows = jnp.concatenate(middles, axis=0)
            squares = squares + rows * rows
    sums = jnp.sum(squares, axis=1, keepdims=True)
    lanes = lax.broadcasted_iota(jnp.int32, (TOK, HD), 1)
    packed = jnp.zeros((TOK, HD), F32)
    for block in range(4):
        column = sums[block * TOK : (block + 1) * TOK]
        coarse = column.astype(BF).astype(F32)
        middle = (column - coarse).astype(BF).astype(F32)
        packed = jnp.where(lanes == block, coarse, packed)
        packed = jnp.where(lanes == block + 32, middle, packed)
        packed = jnp.where(lanes == block + 64, column - coarse - middle, packed)
    for block in range(4):
        attended[block][NQ] = packed.astype(BF)


def digits(ids):
    row = lax.broadcasted_iota(jnp.int32, (16, TXT), 0)
    shifts = jnp.where(row == 0, 0, jnp.where(row == 1, 8, 16))
    value = jnp.bitwise_and(lax.shift_right_logical(jnp.broadcast_to(ids, (16, TXT)), shifts), 255)
    return jnp.where(row < 3, value, 0).astype(F32)


def prompt_kernel(
    info_ref, ids_ref, align_ref, gain_ref, text_ref, after_ref, mixed_ref, own_ref, copy_ref, scale_ref, sem
):
    start = pl.multiple_of(info_ref[0] * (NQ * HD), HD)
    copy = pltpu.make_async_copy(text_ref.at[:, :, :, pl.ds(start, NQ * HD)], copy_ref, sem)
    copy.start()
    pairs = lax.broadcasted_iota(jnp.int32, (TXT, TXT), 0) == align_ref[0:1, :]
    chosen = jnp.where(pairs, 1.0, 0.0)
    aligned = jnp.dot(digits(ids_ref[0:1, :]).astype(BF), chosen.astype(BF), preferred_element_type=F32)
    apart = jnp.sum(jnp.abs(aligned - digits(ids_ref[1:2, :])), axis=0, keepdims=True)
    own = jnp.where(apart == 0.0, 0.0, 1.0)
    own_ref[...] = jnp.broadcast_to(own, (8, TXT))
    selection = (chosen * (1.0 - own)).astype(BF)
    scale_ref[...] = jnp.broadcast_to(gain_ref[0:1, pl.ds(start, NQ * HD)].astype(F32), (8, NQ * HD))
    copy.wait()
    mixed_ref[...] = jnp.dot(selection, copy_ref[1, 1], preferred_element_type=F32).astype(BF)


def prompts(info, prompt_ids, word_align, gain, text_kv, after):
    return call(
        prompt_kernel,
        [
            shaped((TXT, NQ * HD)),
            shaped((8, TXT), F32),
            shaped((2, 2, TXT, NQ * HD)),
            shaped((8, NQ * HD), F32),
        ],
        [info],
        [prompt_ids, word_align.reshape(1, TXT), gain.reshape(1, -1)],
        kept=[(text_kv, pltpu.HBM), (after, pl.ANY)],
        scratch=[pltpu.SemaphoreType.DMA],
        flops=2 * TXT * TXT * NQ * HD,
        limit=47,
    )


def pairs_of(info_ref):
    odd = lax.rem(info_ref[1], 2)
    return ((odd, 3 * (1 - odd)), (2 + odd, 1 + odd))


def scores_kernel(info_ref, middle_ref, gain_ref, text_ref, out_ref):
    pairs = pairs_of(info_ref)
    for head in range(NQ):
        columns = slice(head * HD, (head + 1) * HD)
        gain = gain_ref[0:1, columns]
        for side in range(2):
            rows = jnp.concatenate([middle_ref[head, pair[side]] for pair in pairs], axis=0)
            out_ref[side, head] = dot_t((rows * gain).astype(BF), text_ref[0, side, :, columns])


def cross_kernel(info_ref, s0, s1, s2, s3, middle_ref, scores_ref, text_ref, mixed_ref, own_ref, *refs):
    outs, (scale_ref, done_ref) = refs[:4], refs[4:]
    lanes = lax.broadcasted_iota(jnp.int32, (TOK, HD), 1)

    def sums_of(ref):
        packed = ref[NQ].astype(F32)
        return packed + pltpu.roll(packed, HD - 32, 1) + pltpu.roll(packed, HD - 64, 1)

    squares = sums_of(s0)
    for distance, ref in ((1, s1), (2, s2), (3, s3)):
        other = sums_of(ref)
        turned = pltpu.roll(other, HD - distance, 1)
        wrapped = pltpu.roll(other, 4 - distance, 1)
        squares = squares + jnp.where(lanes < 4 - distance, turned, wrapped)
    norm = lax.rsqrt(squares * (1.0 / (4 * NQ * HD)) + 1e-06) * (SCALE * LOG2E)
    for block in range(4):
        scale_ref[block] = jnp.broadcast_to(norm[:, block : block + 1], (TOK, HD))
    pairs = pairs_of(info_ref)
    own = own_ref[0:1, :]
    norms = [
        jnp.concatenate([scale_ref[pair[side]] for pair in pairs], axis=0)[:, 0:1] for side in range(2)
    ]

    def softmax(side, head):
        scores = scores_ref[side, head] * norms[side]
        weights = jnp.exp2(scores - jnp.max(scores, axis=1, keepdims=True))
        return weights * (1.0 / jnp.sum(weights, axis=1, keepdims=True))

    for head in range(NQ):
        columns = slice(head * HD, (head + 1) * HD)
        source = softmax(0, head).astype(BF)
        edited = (softmax(1, head) * own).astype(BF)
        results = (
            jnp.dot(source, text_ref[1, 0, :, columns], preferred_element_type=F32),
            jnp.dot(source, mixed_ref[:, columns], preferred_element_type=F32)
            + jnp.dot(edited, text_ref[1, 1, :, columns], preferred_element_type=F32),
        )
        for side in range(2):
            for index, pair in enumerate(pairs):
                part = results[side][index * TOK : (index + 1) * TOK]
                done_ref[pair[side]] = middle_ref[head, pair[side]] + part
        for block in range(4):
            outs[block][head] = done_ref[block].astype(BF)


def per_device(queries, keys_values, residual_in, cross_gain, text_kv, prompt_ids, word_align):
    plane = 2 * lax.axis_index("yh") + lax.axis_index("yl")
    quarter = 2 * lax.axis_index("yl") + lax.axis_index("yh")
    where = plane.reshape(1).astype(jnp.int32)
    info = jnp.stack([quarter, plane]).astype(jnp.int32)
    piece = (NQ, TOK, HD)

    kept, first, last, over, mine = call(
        split_kernel,
        [shaped((2 * NQ, TOK, HD)), shaped(piece), shaped(piece), shaped((3 * NQ, TOK, HD)), shaped(piece)],
        [where],
        [queries[0], keys_values],
    )
    over = shift(over, PLANE, 2, 4)
    first = shift(first, PLANE, 1, 4)
    last = shift(last, PLANE, 3, 4)
    residuals = call(split_rows_kernel, [shaped(piece)] * 4, [where], [residual_in[0]])
    residuals = [p if d == 0 else shift(p, PLANE, d, 4) for d, p in enumerate(residuals)]
    buffers = [shaped((count * ROWS, HD)) for _, count, _, _ in GROUPS for _ in range(2)]
    packed = call(pack_kernel, buffers, [], [kept, mine, first, over, last])
    partials, groups = [], []
    for group, (_, count, row_axis, key_axis) in enumerate(GROUPS):
        rows, keys = packed[2 * group], packed[2 * group + 1]
        keys = [keys] + [shift(keys, key_axis, d, 4) for d in (2, 1, 3)]
        rows = [rows] + [shift(rows, row_axis, d, 4) for d in (2, 1, 3)]
        held = call(repack_kernel, [shaped((4 * count * ROWS, HD))], [], keys)[0]
        groups.append((rows, keys, shift(held, "c", 1, 2)))
    for group, (_, _, row_axis, _) in enumerate(GROUPS):
        outs = attend(group, *groups[group])
        partials += [outs[0]] + [shift(outs[i], row_axis, -d, 4) for i, d in ((1, 2), (2, 1), (3, 3))]
    mixed, own, text, gain = prompts(info, prompt_ids, word_align, cross_gain, text_kv, outs[0])
    combined = call(
        combine_kernel,
        [shaped((NQ + 1, TOK, HD))] * 4 + [shaped((NQ, 4, TOK, HD), F32)],
        [],
        [*partials, *residuals],
        kept=[(own, pl.ANY)],
        scratch=[pltpu.VMEM((HD, 2 * HD), F32)],
    )
    middle = combined[4]

    def home(pieces):
        return [p if d == 0 else shift(p, PLANE, -d, 4) for d, p in enumerate(pieces)]

    def join(pieces):
        return call(join_rows_kernel, [shaped((TOK, 4 * NQ * HD))], [where], pieces)[0]

    attended = home(combined[:4])
    scores = call(
        scores_kernel,
        [shaped((2, NQ, KEYS, TXT), F32)],
        [info],
        [middle, gain, text],
        flops=2 * 2 * KEYS * TXT * NQ * HD,
    )[0]
    results = call(
        cross_kernel,
        [shaped(piece)] * 4,
        [info],
        [*attended, middle, scores, text, mixed, own],
        scratch=[pltpu.VMEM((4, TOK, HD), F32), pltpu.VMEM((4, TOK, HD), F32)],
        flops=2 * 3 * KEYS * TXT * NQ * HD,
        exps=2 * KEYS * NQ * TXT,
    )
    results = home(results)
    return (join(attended)[None], join(results)[None])


def solution(mesh):
    grid = Mesh(mesh.devices.reshape(4, 2, 4, 2, 2), ("z", "yh", "x", "c", "yl"))
    seq = ("z", "yh", "x", "c")
    in_specs = (
        P("yl", seq, None),
        P(None, seq, "yl"),
        P("yl", seq, None),
        P(),
        P(),
        P(),
        P(),
    )
    out_specs = (P("yl", seq, None), P("yl", seq, None))
    return jax.shard_map(per_device, mesh=grid, in_specs=in_specs, out_specs=out_specs, check_vma=False)
```

```python
import functools
import math

import jax
import jax.numpy as jnp
from jax import lax
from jax.experimental import pallas as pl
from jax.experimental.pallas import tpu as pltpu
from jax.sharding import Mesh, PartitionSpec as P


HD = 128
NQ = 5
TOK = 56
ROWS = 4 * TOK
KEYS = 2 * TOK
TXT = 512
GROUPS = ((0, 3, "x", "z"), (3, 2, "z", "x"))
STAT = 32
SCALE = 1.0 / math.sqrt(HD)
LOG2E = 1.4426950408889634
PLANE = ("yh", "yl")
BF = jnp.bfloat16
F32 = jnp.float32


def shift(value, axis, distance, size):
    return lax.ppermute(value, axis, [(i, (i + distance) % size) for i in range(size)])


def dot_t(left, right):
    return lax.dot_general(left, right, (((1,), (1,)), ((), ())), preferred_element_type=F32)


def first_head(plane):
    return 10 * (plane % 2) + 5 * (plane // 2)


def vmem(count):
    return [pl.BlockSpec(memory_space=pltpu.VMEM) for _ in range(count)]


def call(kernel, out_shapes, scalars, operands, kept=(), scratch=(), flops=0, exps=0, limit=40):
    in_specs = [pl.BlockSpec(memory_space=pltpu.SMEM)] * len(scalars) + vmem(len(operands))
    in_specs += [pl.BlockSpec(memory_space=space) for _, space in kept]
    moved = sum(math.prod(o.shape) * o.dtype.itemsize for o in operands)
    moved += sum(math.prod(o.shape) * o.dtype.itemsize for o in out_shapes)
    return pl.pallas_call(
        kernel,
        out_shape=out_shapes,
        in_specs=in_specs,
        out_specs=vmem(len(out_shapes)),
        scratch_shapes=list(scratch),
        cost_estimate=pl.CostEstimate(flops=flops, bytes_accessed=moved, transcendentals=exps),
        compiler_params=pltpu.CompilerParams(vmem_limit_bytes=limit << 20),
    )(*scalars, *operands, *(array for array, _ in kept))


def shaped(shape, dtype=BF):
    return jax.ShapeDtypeStruct(shape, dtype)


def stacked(parts):
    return jnp.concatenate([part.astype(F32) for part in parts], axis=0).astype(BF)


def split_kernel(plane_ref, rows_ref, kv_ref, kept, first, last, across, own):
    high = plane_ref[0] // 2
    outs = (own, first, across, last)
    for distance in range(4):
        plane = lax.rem(plane_ref[0] + distance, 4)
        for head in range(NQ):
            lane = pl.multiple_of((first_head(plane) + head) * HD, HD)
            outs[distance][head] = rows_ref[:, pl.ds(lane, HD)]
    for head in range(NQ):
        here = pl.multiple_of((high * NQ + head) * HD, HD)
        there = pl.multiple_of(((1 - high) * NQ + head) * HD, HD)
        for which in range(2):
            kept[2 * head + which] = kv_ref[which, :, pl.ds(here, HD)]
            across[NQ + 2 * head + which] = kv_ref[which, :, pl.ds(there, HD)]


def split_rows_kernel(plane_ref, rows_ref, *outs):
    for distance in range(4):
        plane = lax.rem(plane_ref[0] + distance, 4)
        for head in range(NQ):
            lane = pl.multiple_of((first_head(plane) + head) * HD, HD)
            outs[distance][head] = rows_ref[:, pl.ds(lane, HD)]


def pack_kernel(kept, own, first, across, last, along_x, along_z):
    queries = (own, first, across, last)
    for group, (low, count, _, _) in enumerate(GROUPS):
        rows, keys = (along_x, along_z) if group == 0 else (along_z, along_x)
        for head in range(low, low + count):
            rows[head * ROWS : (head + 1) * ROWS, :] = stacked([query[head] for query in queries])
            keys[head * ROWS : (head + 1) * ROWS, :] = stacked(
                [kept[2 * head], across[NQ + 2 * head], kept[2 * head + 1], across[NQ + 2 * head + 1]]
            )


def repack_kernel(*refs):
    from_x, from_z, out = refs[:4], refs[4:8], refs[9]
    for index in range(4):
        for (low, count, _, _), ref in zip(GROUPS, (from_z[index], from_x[index])):
            start = 4 * low * ROWS + index * count * ROWS
            out[start : start + count * ROWS, :] = ref[low * ROWS : (low + count) * ROWS, :]


def join_rows_kernel(plane_ref, *refs):
    pieces, out = refs[:-1], refs[-1]
    for distance in range(4):
        plane = lax.rem(plane_ref[0] + distance, 4)
        for head in range(NQ):
            lane = pl.multiple_of((first_head(plane) + head) * HD, HD)
            out[:, pl.ds(lane, HD)] = pieces[distance][head]


def attend_kernel(low, count, *refs):
    rows_of, keys_of, swapped = refs[:4], refs[4:8], refs[8]
    outs, (keys, values, stats) = refs[9:13], refs[13:]
    size = count * ROWS
    pieces = [(ref, low * ROWS) for ref in keys_of]
    pieces += [(swapped, 4 * low * ROWS + index * size) for index in range(4)]
    lanes = lax.broadcasted_iota(jnp.int32, (ROWS, HD), 1)
    stats[...] = jnp.zeros_like(stats)

    def one_head(head, _):
        for index, (piece, base) in enumerate(pieces):
            start = pl.multiple_of(base + head * ROWS, 16)
            keys[pl.ds(index * KEYS, KEYS), :] = piece[pl.ds(start, KEYS), :]
            values[pl.ds(index * KEYS, KEYS), :] = piece[
                pl.ds(pl.multiple_of(start + KEYS, 16), KEYS), :
            ]
        for index in range(4):
            start = pl.multiple_of(low * ROWS + head * ROWS, 16)
            scores = dot_t(rows_of[index][pl.ds(start, ROWS), :], keys[...])
            peak = jnp.max(scores, axis=1, keepdims=True)
            weights = jnp.exp2(scores * (SCALE * LOG2E) - peak * (SCALE * LOG2E))
            total = jnp.sum(weights, axis=1, keepdims=True)
            summed = jnp.dot(weights.astype(BF), values[...], preferred_element_type=F32)
            outs[index][pl.ds(pl.multiple_of(head * ROWS, 16), ROWS), :] = (summed / total).astype(BF)
            level = peak * SCALE + jnp.log(total)
            coarse = level.astype(BF).astype(F32)
            middle = (level - coarse).astype(BF).astype(F32)
            fine = level - coarse - middle
            old = stats[index, 0:ROWS, :]
            old = jnp.where(lanes == 3 * head, coarse, old)
            old = jnp.where(lanes == 3 * head + 1, middle, old)
            stats[index, 0:ROWS, :] = jnp.where(lanes == 3 * head + 2, fine, old)
        return 0

    lax.fori_loop(0, count, one_head, 0)
    for index in range(4):
        turned = stats[index].T
        outs[index][size : size + 16, :] = turned[0:16, 0:HD].astype(BF)
        outs[index][size + 16 : size + STAT, :] = turned[0:16, HD : 2 * HD].astype(BF)


def attend(group, rows, keys, swapped):
    low, count, _, _ = GROUPS[group]
    return call(
        functools.partial(attend_kernel, low, count),
        [shaped((count * ROWS + STAT, HD))] * 4,
        [],
        [*rows, *keys, swapped],
        scratch=[
            pltpu.VMEM((8 * KEYS, HD), BF),
            pltpu.VMEM((8 * KEYS, HD), BF),
            pltpu.VMEM((4, 2 * HD, HD), F32),
        ],
        flops=4 * count * 4 * ROWS * 8 * KEYS * HD,
        exps=count * 4 * ROWS * 8 * KEYS,
    )


def combine_kernel(*refs):
    partials = (refs[:4], refs[4:8])
    residuals, attended = refs[8:12], refs[12:16]
    middle_ref, turn_ref = refs[16:]
    turn_ref[...] = jnp.zeros_like(turn_ref)
    squares = jnp.zeros((ROWS, HD), F32)
    for group, (low, count, _, _) in enumerate(GROUPS):
        size = count * ROWS
        levels = []
        for partial in partials[group]:
            turn_ref[0:16, 0:HD] = partial[size : size + 16, :].astype(F32)
            turn_ref[0:16, HD : 2 * HD] = partial[size + 16 : size + STAT, :].astype(F32)
            stat = turn_ref[...].T[0:ROWS, :]
            levels.append(stat + pltpu.roll(stat, HD - 1, 1) + pltpu.roll(stat, HD - 2, 1))
        peak = functools.reduce(jnp.maximum, levels)
        shares = [jnp.exp(level - peak) for level in levels]
        inverse = 1.0 / sum(shares)
        shares = [share * inverse for share in shares]
        for index in range(count):
            head = low + index
            total = sum(
                partial[index * ROWS : (index + 1) * ROWS, :].astype(F32)
                * share[:, 3 * index : 3 * index + 1]
                for partial, share in zip(partials[group], shares)
            )
            middles = []
            for block in range(4):
                part = total[block * TOK : (block + 1) * TOK].astype(BF)
                attended[block][head] = part
                middle = residuals[block][head].astype(F32) + part.astype(F32)
                middle_ref[head, block] = middle
                middles.append(middle)
            rows = jnp.concatenate(middles, axis=0)
            squares = squares + rows * rows
    sums = jnp.sum(squares, axis=1, keepdims=True)
    lanes = lax.broadcasted_iota(jnp.int32, (TOK, HD), 1)
    packed = jnp.zeros((TOK, HD), F32)
    for block in range(4):
        column = sums[block * TOK : (block + 1) * TOK]
        coarse = column.astype(BF).astype(F32)
        middle = (column - coarse).astype(BF).astype(F32)
        packed = jnp.where(lanes == block, coarse, packed)
        packed = jnp.where(lanes == block + 32, middle, packed)
        packed = jnp.where(lanes == block + 64, column - coarse - middle, packed)
    for block in range(4):
        attended[block][NQ] = packed.astype(BF)


def digits(ids):
    row = lax.broadcasted_iota(jnp.int32, (16, TXT), 0)
    shifts = jnp.where(row == 0, 0, jnp.where(row == 1, 8, 16))
    value = jnp.bitwise_and(lax.shift_right_logical(jnp.broadcast_to(ids, (16, TXT)), shifts), 255)
    return jnp.where(row < 3, value, 0).astype(F32)


def prompt_kernel(
    info_ref, ids_ref, align_ref, gain_ref, text_ref, mixed_ref, own_ref, copy_ref, scale_ref, sem
):
    start = pl.multiple_of(info_ref[0] * (NQ * HD), HD)
    copy = pltpu.make_async_copy(text_ref.at[:, :, :, pl.ds(start, NQ * HD)], copy_ref, sem)
    copy.start()
    pairs = lax.broadcasted_iota(jnp.int32, (TXT, TXT), 0) == align_ref[0:1, :]
    chosen = jnp.where(pairs, 1.0, 0.0)
    aligned = jnp.dot(digits(ids_ref[0:1, :]).astype(BF), chosen.astype(BF), preferred_element_type=F32)
    apart = jnp.sum(jnp.abs(aligned - digits(ids_ref[1:2, :])), axis=0, keepdims=True)
    own = jnp.where(apart == 0.0, 0.0, 1.0)
    own_ref[...] = jnp.broadcast_to(own, (8, TXT))
    selection = (chosen * (1.0 - own)).astype(BF)
    scale_ref[...] = jnp.broadcast_to(gain_ref[0:1, pl.ds(start, NQ * HD)].astype(F32), (8, NQ * HD))
    copy.wait()
    mixed_ref[...] = jnp.dot(selection, copy_ref[1, 1], preferred_element_type=F32).astype(BF)


def prompts(info, prompt_ids, word_align, gain, text_kv):
    return call(
        prompt_kernel,
        [
            shaped((TXT, NQ * HD)),
            shaped((8, TXT), F32),
            shaped((2, 2, TXT, NQ * HD)),
            shaped((8, NQ * HD), F32),
        ],
        [info],
        [prompt_ids, word_align.reshape(1, TXT), gain.reshape(1, -1)],
        kept=[(text_kv, pltpu.HBM)],
        scratch=[pltpu.SemaphoreType.DMA],
        flops=2 * TXT * TXT * NQ * HD,
        limit=47,
    )


def pairs_of(info_ref):
    odd = lax.rem(info_ref[1], 2)
    return ((odd, 3 * (1 - odd)), (2 + odd, 1 + odd))


def scores_kernel(info_ref, middle_ref, gain_ref, text_ref, out_ref):
    pairs = pairs_of(info_ref)
    for head in range(NQ):
        columns = slice(head * HD, (head + 1) * HD)
        gain = gain_ref[0:1, columns]
        for side in range(2):
            rows = jnp.concatenate([middle_ref[head, pair[side]] for pair in pairs], axis=0)
            out_ref[side, head] = dot_t((rows * gain).astype(BF), text_ref[0, side, :, columns])


def cross_kernel(info_ref, s0, s1, s2, s3, middle_ref, scores_ref, text_ref, mixed_ref, own_ref, *refs):
    outs, (scale_ref, done_ref) = refs[:4], refs[4:]
    lanes = lax.broadcasted_iota(jnp.int32, (TOK, HD), 1)

    def sums_of(ref):
        packed = ref[NQ].astype(F32)
        return packed + pltpu.roll(packed, HD - 32, 1) + pltpu.roll(packed, HD - 64, 1)

    squares = sums_of(s0)
    for distance, ref in ((1, s1), (2, s2), (3, s3)):
        other = sums_of(ref)
        turned = pltpu.roll(other, HD - distance, 1)
        wrapped = pltpu.roll(other, 4 - distance, 1)
        squares = squares + jnp.where(lanes < 4 - distance, turned, wrapped)
    norm = lax.rsqrt(squares * (1.0 / (4 * NQ * HD)) + 1e-06) * (SCALE * LOG2E)
    for block in range(4):
        scale_ref[block] = jnp.broadcast_to(norm[:, block : block + 1], (TOK, HD))
    pairs = pairs_of(info_ref)
    own = own_ref[0:1, :]
    norms = [
        jnp.concatenate([scale_ref[pair[side]] for pair in pairs], axis=0)[:, 0:1] for side in range(2)
    ]

    def softmax(side, head):
        scores = scores_ref[side, head] * norms[side]
        weights = jnp.exp2(scores - jnp.max(scores, axis=1, keepdims=True))
        return weights * (1.0 / jnp.sum(weights, axis=1, keepdims=True))

    for head in range(NQ):
        columns = slice(head * HD, (head + 1) * HD)
        source = softmax(0, head).astype(BF)
        edited = (softmax(1, head) * own).astype(BF)
        results = (
            jnp.dot(source, text_ref[1, 0, :, columns], preferred_element_type=F32),
            jnp.dot(source, mixed_ref[:, columns], preferred_element_type=F32)
            + jnp.dot(edited, text_ref[1, 1, :, columns], preferred_element_type=F32),
        )
        for side in range(2):
            for index, pair in enumerate(pairs):
                part = results[side][index * TOK : (index + 1) * TOK]
                done_ref[pair[side]] = middle_ref[head, pair[side]] + part
        for block in range(4):
            outs[block][head] = done_ref[block].astype(BF)


def per_device(queries, keys_values, residual_in, cross_gain, text_kv, prompt_ids, word_align):
    plane = 2 * lax.axis_index("yh") + lax.axis_index("yl")
    quarter = 2 * lax.axis_index("yl") + lax.axis_index("yh")
    where = plane.reshape(1).astype(jnp.int32)
    info = jnp.stack([quarter, plane]).astype(jnp.int32)
    piece = (NQ, TOK, HD)

    kept, first, last, over, mine = call(
        split_kernel,
        [shaped((2 * NQ, TOK, HD)), shaped(piece), shaped(piece), shaped((3 * NQ, TOK, HD)), shaped(piece)],
        [where],
        [queries[0], keys_values],
    )
    over = shift(over, PLANE, 2, 4)
    first = shift(first, PLANE, 1, 4)
    last = shift(last, PLANE, 3, 4)
    residuals = call(split_rows_kernel, [shaped(piece)] * 4, [where], [residual_in[0]])
    residuals = [p if d == 0 else shift(p, PLANE, d, 4) for d, p in enumerate(residuals)]
    buffer = shaped((NQ * ROWS, HD))
    along_x, along_z = call(pack_kernel, [buffer] * 2, [], [kept, mine, first, over, last])
    from_x = [along_x] + [shift(along_x, "x", d, 4) for d in (2, 1, 3)]
    from_z = [along_z] + [shift(along_z, "z", d, 4) for d in (2, 1, 3)]
    mixed, own, text, gain = prompts(info, prompt_ids, word_align, cross_gain, text_kv)
    held = call(repack_kernel, [shaped((4 * NQ * ROWS, HD))], [], [*from_x, *from_z], kept=[(own, pl.ANY)])[0]
    swapped = shift(held, "c", 1, 2)
    groups = ((from_x, from_z, swapped), (from_z, from_x, swapped))
    partials = []
    for group, (_, _, row_axis, _) in enumerate(GROUPS):
        outs = attend(group, *groups[group])
        partials += [outs[0]] + [shift(outs[i], row_axis, -d, 4) for i, d in ((1, 2), (2, 1), (3, 3))]
    combined = call(
        combine_kernel,
        [shaped((NQ + 1, TOK, HD))] * 4 + [shaped((NQ, 4, TOK, HD), F32)],
        [],
        [*partials, *residuals],
        scratch=[pltpu.VMEM((HD, 2 * HD), F32)],
    )
    middle = combined[4]

    def home(pieces):
        return [p if d == 0 else shift(p, PLANE, -d, 4) for d, p in enumerate(pieces)]

    def join(pieces):
        return call(join_rows_kernel, [shaped((TOK, 4 * NQ * HD))], [where], pieces)[0]

    attended = home(combined[:4])
    scores = call(
        scores_kernel,
        [shaped((2, NQ, KEYS, TXT), F32)],
        [info],
        [middle, gain, text],
        flops=2 * 2 * KEYS * TXT * NQ * HD,
    )[0]
    results = call(
        cross_kernel,
        [shaped(piece)] * 4,
        [info],
        [*attended, middle, scores, text, mixed, own],
        scratch=[pltpu.VMEM((4, TOK, HD), F32), pltpu.VMEM((4, TOK, HD), F32)],
        flops=2 * 3 * KEYS * TXT * NQ * HD,
        exps=2 * KEYS * NQ * TXT,
    )
    results = home(results)
    return (join(attended)[None], join(results)[None])


def solution(mesh):
    grid = Mesh(mesh.devices.reshape(4, 2, 4, 2, 2), ("z", "yh", "x", "c", "yl"))
    seq = ("z", "yh", "x", "c")
    in_specs = (
        P("yl", seq, None),
        P(None, seq, "yl"),
        P("yl", seq, None),
        P(),
        P(),
        P(),
        P(),
    )
    out_specs = (P("yl", seq, None), P("yl", seq, None))
    return jax.shard_map(per_device, mesh=grid, in_specs=in_specs, out_specs=out_specs, check_vma=False)
```

```python
import functools
import math

import jax
import jax.numpy as jnp
from jax import lax
from jax.experimental import pallas as pl
from jax.experimental.pallas import tpu as pltpu
from jax.sharding import Mesh, PartitionSpec as P


HD = 128
NQ = 5
TOK = 56
ROWS = 4 * TOK
KEYS = 2 * TOK
TXT = 512
GROUPS = ((0, 3, "x", "z"), (3, 2, "z", "x"))
STAT = 32
SCALE = 1.0 / math.sqrt(HD)
LOG2E = 1.4426950408889634
PLANE = ("yh", "yl")
BF = jnp.bfloat16
F32 = jnp.float32


def shift(value, axis, distance, size):
    return lax.ppermute(value, axis, [(i, (i + distance) % size) for i in range(size)])


def dot_t(left, right):
    return lax.dot_general(left, right, (((1,), (1,)), ((), ())), preferred_element_type=F32)


def first_head(plane):
    return 10 * (plane % 2) + 5 * (plane // 2)


def vmem(count):
    return [pl.BlockSpec(memory_space=pltpu.VMEM) for _ in range(count)]


def call(kernel, out_shapes, scalars, operands, kept=(), scratch=(), flops=0, exps=0, limit=16):
    in_specs = [pl.BlockSpec(memory_space=pltpu.SMEM)] * len(scalars) + vmem(len(operands))
    in_specs += [pl.BlockSpec(memory_space=space) for _, space in kept]
    moved = sum(math.prod(o.shape) * o.dtype.itemsize for o in operands)
    moved += sum(math.prod(o.shape) * o.dtype.itemsize for o in out_shapes)
    return pl.pallas_call(
        kernel,
        out_shape=out_shapes,
        in_specs=in_specs,
        out_specs=vmem(len(out_shapes)),
        scratch_shapes=list(scratch),
        cost_estimate=pl.CostEstimate(flops=flops, bytes_accessed=moved, transcendentals=exps),
        compiler_params=pltpu.CompilerParams(vmem_limit_bytes=limit << 20),
    )(*scalars, *operands, *(array for array, _ in kept))


def shaped(shape, dtype=BF):
    return jax.ShapeDtypeStruct(shape, dtype)


def stacked(parts):
    return jnp.concatenate([part.astype(F32) for part in parts], axis=0).astype(BF)


LOW, WIDE, NARROW = GROUPS[1][0], GROUPS[0][1], GROUPS[1][1]


def split_kernel(plane_ref, rows_ref, kv_ref, along_x, along_z, first, last, across):
    high = plane_ref[0] // 2
    for distance in range(4):
        plane = lax.rem(plane_ref[0] + distance, 4)
        for head in range(NQ):
            lane = pl.multiple_of((first_head(plane) + head) * HD, HD)
            rows = rows_ref[:, pl.ds(lane, HD)]
            if distance == 0 and head < LOW:
                along_x[head] = rows
            elif distance == 0:
                along_z[2 * WIDE + head - LOW] = rows
            else:
                (first, across, last)[distance - 1][head] = rows
    for head in range(NQ):
        here = pl.multiple_of((high * NQ + head) * HD, HD)
        there = pl.multiple_of(((1 - high) * NQ + head) * HD, HD)
        for which in range(2):
            rows = kv_ref[which, :, pl.ds(here, HD)]
            if head < LOW:
                along_z[2 * head + which] = rows
            else:
                along_x[WIDE + 2 * (head - LOW) + which] = rows
            across[NQ + 2 * head + which] = kv_ref[which, :, pl.ds(there, HD)]


def pack_kernel(first, across, last, along_x, along_z):
    for head in range(NQ):
        for index, query in enumerate((first, across, last)):
            if head < LOW:
                along_x[3 * head + index] = query[head]
            else:
                along_z[2 * WIDE + 3 * (head - LOW) + index] = query[head]
        for which in range(2):
            rows = across[NQ + 2 * head + which]
            if head < LOW:
                along_z[2 * head + which] = rows
            else:
                along_x[3 * WIDE + 2 * (head - LOW) + which] = rows


def order_kernel(*refs):
    x1, z1, x2, z2, out, rows = refs[:4], refs[4:8], refs[8:12], refs[12:16], refs[16], refs[17]
    for head in range(NQ):
        for which in range(2):
            for index in range(4):
                if head < LOW:
                    unit = 2 * head + which
                    parts = [z1[index][unit], z2[index][unit]]
                else:
                    unit = 2 * (head - LOW) + which
                    parts = [x1[index][WIDE + unit], x2[index][3 * WIDE + unit]]
                out[2 * head + which, index * KEYS : (index + 1) * KEYS, :] = stacked(parts)

    for head in range(NQ):
        for index in range(4):
            if head < LOW:
                parts = [x1[index][head]] + [x2[index][3 * head + k] for k in range(3)]
            else:
                unit = head - LOW
                parts = [z1[index][2 * WIDE + unit]]
                parts += [z2[index][2 * WIDE + 3 * unit + k] for k in range(3)]
            rows[head, index * ROWS : (index + 1) * ROWS, :] = stacked(parts)


def split_rows_kernel(plane_ref, rows_ref, *outs):
    for distance in range(4):
        plane = lax.rem(plane_ref[0] + distance, 4)
        for head in range(NQ):
            lane = pl.multiple_of((first_head(plane) + head) * HD, HD)
            outs[distance][head] = rows_ref[:, pl.ds(lane, HD)]


def join_rows_kernel(plane_ref, *refs):
    pieces, out = refs[:-1], refs[-1]
    for distance in range(4):
        plane = lax.rem(plane_ref[0] + distance, 4)
        for head in range(NQ):
            lane = pl.multiple_of((first_head(plane) + head) * HD, HD)
            out[:, pl.ds(lane, HD)] = pieces[distance][head]


def attend_kernel(low, count, queries, held, swapped, *refs):
    outs, (peaks, totals) = refs[:4], refs[4:]
    size = count * ROWS
    lanes = lax.broadcasted_iota(jnp.int32, (ROWS, HD), 1)
    peaks[...] = jnp.zeros_like(peaks)
    totals[...] = jnp.ones_like(totals)
    tiles = [(head, index) for head in range(count) for index in range(4)]

    def whole(head, which):
        unit = 2 * (low + head) + which
        return jnp.concatenate([held[unit], swapped[unit]], axis=0)

    def scores_of(head, index):
        return dot_t(queries[low + head, index * ROWS : (index + 1) * ROWS, :], whole(head, 0))

    scores = scores_of(*tiles[0])
    for step, (head, index) in enumerate(tiles):
        ahead = scores_of(*tiles[step + 1]) if step + 1 < len(tiles) else None
        peak = jnp.max(scores, axis=1, keepdims=True)
        weights = jnp.exp2(scores * (SCALE * LOG2E) - peak * (SCALE * LOG2E))
        total = jnp.sum(weights, axis=1, keepdims=True)
        summed = jnp.dot(weights.astype(BF), whole(head, 1), preferred_element_type=F32)
        outs[index][head * ROWS : (head + 1) * ROWS, :] = (summed * (1.0 / total)).astype(BF)
        peaks[index, 0:ROWS, :] = jnp.where(lanes == head, peak, peaks[index, 0:ROWS, :])
        totals[index, 0:ROWS, :] = jnp.where(lanes == head, total, totals[index, 0:ROWS, :])
        scores = ahead
    for index in range(4):
        level = peaks[index] * SCALE + jnp.log(totals[index])
        coarse = level.astype(BF).astype(F32)
        middle = (level - coarse).astype(BF).astype(F32)
        fine = level - coarse - middle
        places = lax.broadcasted_iota(jnp.int32, level.shape, 1)
        parts = jnp.where(places < NQ, coarse, pltpu.roll(middle, NQ, 1))
        turned = jnp.where(places < 2 * NQ, parts, pltpu.roll(fine, 2 * NQ, 1)).T
        outs[index][size : size + 16, :] = turned[0:16, 0:HD].astype(BF)
        outs[index][size + 16 : size + STAT, :] = turned[0:16, HD : 2 * HD].astype(BF)


def attend(group, queries, held, swapped):
    low, count, _, _ = GROUPS[group]
    return call(
        functools.partial(attend_kernel, low, count),
        [shaped((count * ROWS + STAT, HD))] * 4,
        [],
        [queries, held, swapped],
        scratch=[pltpu.VMEM((4, 2 * HD, HD), F32)] * 2,
        flops=4 * count * 4 * ROWS * 8 * KEYS * HD,
        exps=count * 4 * ROWS * 8 * KEYS,
        limit=32,
    )


def combine_kernel(*refs):
    partials = (refs[:4], refs[4:8])
    residuals, attended = refs[8:12], refs[13:17]
    middle_ref, turn_ref = refs[17:]
    turn_ref[...] = jnp.zeros_like(turn_ref)
    squares = jnp.zeros((ROWS, HD), F32)
    for group, (low, count, _, _) in enumerate(GROUPS):
        size = count * ROWS
        levels = []
        for partial in partials[group]:
            turn_ref[0:16, 0:HD] = partial[size : size + 16, :].astype(F32)
            turn_ref[0:16, HD : 2 * HD] = partial[size + 16 : size + STAT, :].astype(F32)
            stat = turn_ref[...].T[0:ROWS, :]
            levels.append(stat + pltpu.roll(stat, HD - NQ, 1) + pltpu.roll(stat, HD - 2 * NQ, 1))
        peak = functools.reduce(jnp.maximum, levels)
        shares = [jnp.exp(level - peak) for level in levels]
        inverse = 1.0 / sum(shares)
        shares = [share * inverse for share in shares]
        for index in range(count):
            head = low + index
            total = sum(
                partial[index * ROWS : (index + 1) * ROWS, :].astype(F32)
                * share[:, index : index + 1]
                for partial, share in zip(partials[group], shares)
            )
            middles = []
            for block in range(4):
                part = total[block * TOK : (block + 1) * TOK].astype(BF)
                attended[block][head] = part
                middle = residuals[block][head].astype(F32) + part.astype(F32)
                middle_ref[head, block] = middle
                middles.append(middle)
            rows = jnp.concatenate(middles, axis=0)
            squares = squares + rows * rows
    sums = jnp.sum(squares, axis=1, keepdims=True)
    lanes = lax.broadcasted_iota(jnp.int32, (TOK, HD), 1)
    packed = jnp.zeros((TOK, HD), F32)
    for block in range(4):
        column = sums[block * TOK : (block + 1) * TOK]
        coarse = column.astype(BF).astype(F32)
        middle = (column - coarse).astype(BF).astype(F32)
        packed = jnp.where(lanes == block, coarse, packed)
        packed = jnp.where(lanes == block + 32, middle, packed)
        packed = jnp.where(lanes == block + 64, column - coarse - middle, packed)
    for block in range(4):
        attended[block][NQ] = packed.astype(BF)


def digits(ids):
    row = lax.broadcasted_iota(jnp.int32, (16, TXT), 0)
    shifts = jnp.where(row == 0, 0, jnp.where(row == 1, 8, 16))
    value = jnp.bitwise_and(lax.shift_right_logical(jnp.broadcast_to(ids, (16, TXT)), shifts), 255)
    return jnp.where(row < 3, value, 0).astype(F32)


def prompt_kernel(
    info_ref, ids_ref, align_ref, gain_ref, text_ref, after_ref, mixed_ref, own_ref, copy_ref, scale_ref, sem
):
    start = pl.multiple_of(info_ref[0] * (NQ * HD), HD)
    copy = pltpu.make_async_copy(text_ref.at[:, :, :, pl.ds(start, NQ * HD)], copy_ref, sem)
    copy.start()
    pairs = lax.broadcasted_iota(jnp.int32, (TXT, TXT), 0) == align_ref[0:1, :]
    chosen = jnp.where(pairs, 1.0, 0.0)
    aligned = jnp.dot(digits(ids_ref[0:1, :]).astype(BF), chosen.astype(BF), preferred_element_type=F32)
    apart = jnp.sum(jnp.abs(aligned - digits(ids_ref[1:2, :])), axis=0, keepdims=True)
    own = jnp.where(apart == 0.0, 0.0, 1.0)
    own_ref[...] = jnp.broadcast_to(own, (8, TXT))
    selection = (chosen * (1.0 - own)).astype(BF)
    scale_ref[...] = jnp.broadcast_to(gain_ref[0:1, pl.ds(start, NQ * HD)].astype(F32), (8, NQ * HD))
    copy.wait()
    mixed_ref[...] = jnp.dot(selection, copy_ref[1, 1], preferred_element_type=F32).astype(BF)


def prompts(info, prompt_ids, word_align, gain, text_kv, after):
    return call(
        prompt_kernel,
        [
            shaped((TXT, NQ * HD)),
            shaped((8, TXT), F32),
            shaped((2, 2, TXT, NQ * HD)),
            shaped((8, NQ * HD), F32),
        ],
        [info],
        [prompt_ids, word_align.reshape(1, TXT), gain.reshape(1, -1)],
        kept=[(text_kv, pltpu.HBM), (after, pl.ANY)],
        scratch=[pltpu.SemaphoreType.DMA],
        flops=2 * TXT * TXT * NQ * HD,
        limit=47,
    )


def pairs_of(info_ref):
    odd = lax.rem(info_ref[1], 2)
    return ((odd, 3 * (1 - odd)), (2 + odd, 1 + odd))


def scores_kernel(info_ref, middle_ref, gain_ref, text_ref, out_ref):
    pairs = pairs_of(info_ref)
    for head in range(NQ):
        columns = slice(head * HD, (head + 1) * HD)
        gain = gain_ref[0:1, columns]
        for side in range(2):
            rows = jnp.concatenate([middle_ref[head, pair[side]] for pair in pairs], axis=0)
            out_ref[side, head] = dot_t((rows * gain).astype(BF), text_ref[0, side, :, columns])


def cross_kernel(info_ref, s0, s1, s2, s3, middle_ref, scores_ref, text_ref, mixed_ref, own_ref, *refs):
    outs, (scale_ref, done_ref) = refs[:4], refs[4:]
    lanes = lax.broadcasted_iota(jnp.int32, (TOK, HD), 1)

    def sums_of(ref):
        packed = ref[NQ].astype(F32)
        return packed + pltpu.roll(packed, HD - 32, 1) + pltpu.roll(packed, HD - 64, 1)

    squares = sums_of(s0)
    for distance, ref in ((1, s1), (2, s2), (3, s3)):
        other = sums_of(ref)
        turned = pltpu.roll(other, HD - distance, 1)
        wrapped = pltpu.roll(other, 4 - distance, 1)
        squares = squares + jnp.where(lanes < 4 - distance, turned, wrapped)
    norm = lax.rsqrt(squares * (1.0 / (4 * NQ * HD)) + 1e-06) * (SCALE * LOG2E)
    for block in range(4):
        scale_ref[block] = jnp.broadcast_to(norm[:, block : block + 1], (TOK, HD))
    pairs = pairs_of(info_ref)
    own = own_ref[0:1, :]
    norms = [
        jnp.concatenate([scale_ref[pair[side]] for pair in pairs], axis=0)[:, 0:1] for side in range(2)
    ]

    def softmax(side, head):
        scores = scores_ref[side, head] * norms[side]
        weights = jnp.exp2(scores - jnp.max(scores, axis=1, keepdims=True))
        return weights * (1.0 / jnp.sum(weights, axis=1, keepdims=True))

    for head in range(NQ):
        columns = slice(head * HD, (head + 1) * HD)
        source = softmax(0, head).astype(BF)
        edited = (softmax(1, head) * own).astype(BF)
        results = (
            jnp.dot(source, text_ref[1, 0, :, columns], preferred_element_type=F32),
            jnp.dot(source, mixed_ref[:, columns], preferred_element_type=F32)
            + jnp.dot(edited, text_ref[1, 1, :, columns], preferred_element_type=F32),
        )
        for side in range(2):
            for index, pair in enumerate(pairs):
                part = results[side][index * TOK : (index + 1) * TOK]
                done_ref[pair[side]] = middle_ref[head, pair[side]] + part
        for block in range(4):
            outs[block][head] = done_ref[block].astype(BF)


def per_device(queries, keys_values, residual_in, cross_gain, text_kv, prompt_ids, word_align):
    plane = 2 * lax.axis_index("yh") + lax.axis_index("yl")
    quarter = 2 * lax.axis_index("yl") + lax.axis_index("yh")
    where = plane.reshape(1).astype(jnp.int32)
    info = jnp.stack([quarter, plane]).astype(jnp.int32)
    piece = (NQ, TOK, HD)

    along_x, along_z, first, last, over = call(
        split_kernel,
        [
            shaped((WIDE + 2 * NARROW, TOK, HD)),
            shaped((2 * WIDE + NARROW, TOK, HD)),
            shaped(piece),
            shaped(piece),
            shaped((3 * NQ, TOK, HD)),
        ],
        [where],
        [queries[0], keys_values],
    )

    def gathered(value, axis):
        return [value] + [shift(value, axis, d, 4) for d in (2, 1, 3)]

    over = shift(over, PLANE, 2, 4)
    first = shift(first, PLANE, 1, 4)
    last = shift(last, PLANE, 3, 4)
    units = gathered(along_x, "x") + gathered(along_z, "z")
    along_x, along_z = call(
        pack_kernel,
        [shaped((3 * WIDE + 2 * NARROW, TOK, HD)), shaped((2 * WIDE + 3 * NARROW, TOK, HD))],
        [],
        [first, over, last],
    )
    units = units + gathered(along_x, "x") + gathered(along_z, "z")
    residuals = call(split_rows_kernel, [shaped(piece)] * 4, [where], [residual_in[0]])
    residuals = [p if d == 0 else shift(p, PLANE, d, 4) for d, p in enumerate(residuals)]
    held, rows = call(
        order_kernel, [shaped((2 * NQ, 4 * KEYS, HD)), shaped((NQ, 4 * ROWS, HD))], [], units
    )
    swapped = shift(held, "c", 1, 2)
    partials = []
    for group, (_, _, row_axis, _) in enumerate(GROUPS):
        outs = attend(group, rows, held, swapped)
        partials += [outs[0]] + [shift(outs[i], row_axis, -d, 4) for i, d in ((1, 2), (2, 1), (3, 3))]
    mixed, own, text, gain = prompts(info, prompt_ids, word_align, cross_gain, text_kv, outs[0])
    combined = call(
        combine_kernel,
        [shaped((NQ + 1, TOK, HD))] * 4 + [shaped((NQ, 4, TOK, HD), F32)],
        [],
        [*partials, *residuals],
        kept=[(own, pl.ANY)],
        scratch=[pltpu.VMEM((HD, 2 * HD), F32)],
    )
    middle = combined[4]

    def home(pieces):
        return [p if d == 0 else shift(p, PLANE, -d, 4) for d, p in enumerate(pieces)]

    def join(pieces):
        return call(join_rows_kernel, [shaped((TOK, 4 * NQ * HD))], [where], pieces)[0]

    attended = home(combined[:4])
    scores = call(
        scores_kernel,
        [shaped((2, NQ, KEYS, TXT), F32)],
        [info],
        [middle, gain, text],
        flops=2 * 2 * KEYS * TXT * NQ * HD,
    )[0]
    results = call(
        cross_kernel,
        [shaped(piece)] * 4,
        [info],
        [*attended, middle, scores, text, mixed, own],
        scratch=[pltpu.VMEM((4, TOK, HD), F32), pltpu.VMEM((4, TOK, HD), F32)],
        flops=2 * 3 * KEYS * TXT * NQ * HD,
        exps=2 * KEYS * NQ * TXT,
        limit=24,
    )
    results = home(results)
    return (join(attended)[None], join(results)[None])


def solution(mesh):
    grid = Mesh(mesh.devices.reshape(4, 2, 4, 2, 2), ("z", "yh", "x", "c", "yl"))
    seq = ("z", "yh", "x", "c")
    in_specs = (
        P("yl", seq, None),
        P(None, seq, "yl"),
        P("yl", seq, None),
        P(),
        P(),
        P(),
        P(),
    )
    out_specs = (P("yl", seq, None), P("yl", seq, None))
    return jax.shard_map(per_device, mesh=grid, in_specs=in_specs, out_specs=out_specs, check_vma=False)
```

```python
import functools
import math

import jax
import jax.numpy as jnp
from jax import lax
from jax.experimental import pallas as pl
from jax.experimental.pallas import tpu as pltpu
from jax.sharding import Mesh, PartitionSpec as P


HD = 128
NQ = 5
TOK = 56
ROWS = 4 * TOK
KEYS = 2 * TOK
TXT = 512
GROUPS = ((0, 3, "x", "z"), (3, 2, "z", "x"))
STAT = 32
SCALE = 1.0 / math.sqrt(HD)
LOG2E = 1.4426950408889634
PLANE = ("yh", "yl")
BF = jnp.bfloat16
F32 = jnp.float32


def shift(value, axis, distance, size):
    return lax.ppermute(value, axis, [(i, (i + distance) % size) for i in range(size)])


def dot_t(left, right):
    return lax.dot_general(left, right, (((1,), (1,)), ((), ())), preferred_element_type=F32)


def first_head(plane):
    return 10 * (plane % 2) + 5 * (plane // 2)


def vmem(count):
    return [pl.BlockSpec(memory_space=pltpu.VMEM) for _ in range(count)]


def call(kernel, out_shapes, scalars, operands, kept=(), scratch=(), flops=0, exps=0, limit=16):
    in_specs = [pl.BlockSpec(memory_space=pltpu.SMEM)] * len(scalars) + vmem(len(operands))
    in_specs += [pl.BlockSpec(memory_space=space) for _, space in kept]
    moved = sum(math.prod(o.shape) * o.dtype.itemsize for o in operands)
    moved += sum(math.prod(o.shape) * o.dtype.itemsize for o in out_shapes)
    return pl.pallas_call(
        kernel,
        out_shape=out_shapes,
        in_specs=in_specs,
        out_specs=vmem(len(out_shapes)),
        scratch_shapes=list(scratch),
        cost_estimate=pl.CostEstimate(flops=flops, bytes_accessed=moved, transcendentals=exps),
        compiler_params=pltpu.CompilerParams(vmem_limit_bytes=limit << 20),
    )(*scalars, *operands, *(array for array, _ in kept))


def shaped(shape, dtype=BF):
    return jax.ShapeDtypeStruct(shape, dtype)


def stacked(parts):
    return jnp.concatenate([part.astype(F32) for part in parts], axis=0).astype(BF)


LOW, WIDE, NARROW = GROUPS[1][0], GROUPS[0][1], GROUPS[1][1]


def split_near_kernel(plane_ref, rows_ref, residual_ref, first, last):
    for out, distance in ((first, 1), (last, 3)):
        plane = lax.rem(plane_ref[0] + distance, 4)
        for head in range(NQ):
            lane = pl.multiple_of((first_head(plane) + head) * HD, HD)
            out[head] = rows_ref[:, pl.ds(lane, HD)]
            out[NQ + head] = residual_ref[:, pl.ds(lane, HD)]


def split_kernel(plane_ref, rows_ref, residual_ref, kv_ref, along_x, along_z, across, residual):
    high = plane_ref[0] // 2
    opposite = lax.rem(plane_ref[0] + 2, 4)
    for head in range(NQ):
        lane = pl.multiple_of((first_head(opposite) + head) * HD, HD)
        across[head] = rows_ref[:, pl.ds(lane, HD)]
        across[NQ + head] = residual_ref[:, pl.ds(lane, HD)]
        lane = pl.multiple_of((first_head(plane_ref[0]) + head) * HD, HD)
        residual[head] = residual_ref[:, pl.ds(lane, HD)]
        rows = rows_ref[:, pl.ds(lane, HD)]
        if head < LOW:
            along_x[head] = rows
        else:
            along_z[2 * WIDE + head - LOW] = rows
        here = pl.multiple_of((high * NQ + head) * HD, HD)
        there = pl.multiple_of(((1 - high) * NQ + head) * HD, HD)
        for which in range(2):
            rows = kv_ref[which, :, pl.ds(here, HD)]
            if head < LOW:
                along_z[2 * head + which] = rows
            else:
                along_x[WIDE + 2 * (head - LOW) + which] = rows
            across[2 * NQ + 2 * head + which] = kv_ref[which, :, pl.ds(there, HD)]


def pack_kernel(first, across, last, along_x, along_z):
    for head in range(NQ):
        for index, query in enumerate((first, across, last)):
            if head < LOW:
                along_x[3 * head + index] = query[head]
            else:
                along_z[2 * WIDE + 3 * (head - LOW) + index] = query[head]
        for which in range(2):
            rows = across[2 * NQ + 2 * head + which]
            if head < LOW:
                along_z[2 * head + which] = rows
            else:
                along_x[3 * WIDE + 2 * (head - LOW) + which] = rows


def order_kernel(*refs):
    x1, z1, x2, z2, out, rows = refs[:4], refs[4:8], refs[8:12], refs[12:16], refs[16], refs[17]
    for head in range(NQ):
        for which in range(2):
            for index in range(4):
                if head < LOW:
                    unit = 2 * head + which
                    parts = [z1[index][unit], z2[index][unit]]
                else:
                    unit = 2 * (head - LOW) + which
                    parts = [x1[index][WIDE + unit], x2[index][3 * WIDE + unit]]
                out[2 * head + which, index * KEYS : (index + 1) * KEYS, :] = stacked(parts)

    for head in range(NQ):
        for index in range(4):
            if head < LOW:
                parts = [x1[index][head]] + [x2[index][3 * head + k] for k in range(3)]
            else:
                unit = head - LOW
                parts = [z1[index][2 * WIDE + unit]]
                parts += [z2[index][2 * WIDE + 3 * unit + k] for k in range(3)]
            rows[head, index * ROWS : (index + 1) * ROWS, :] = stacked(parts)


def join_rows_kernel(plane_ref, *refs):
    pieces, out = refs[:-1], refs[-1]
    for distance in range(4):
        plane = lax.rem(plane_ref[0] + distance, 4)
        for head in range(NQ):
            lane = pl.multiple_of((first_head(plane) + head) * HD, HD)
            out[:, pl.ds(lane, HD)] = pieces[distance][head]


def attend_kernel(low, count, queries, held, swapped, *refs):
    outs, (peaks, totals) = refs[:4], refs[4:]
    size = count * ROWS
    lanes = lax.broadcasted_iota(jnp.int32, (ROWS, HD), 1)
    peaks[...] = jnp.zeros_like(peaks)
    totals[...] = jnp.ones_like(totals)
    tiles = [(head, index) for head in range(count) for index in range(4)]

    def whole(head, which):
        unit = 2 * (low + head) + which
        return jnp.concatenate([held[unit], swapped[unit]], axis=0)

    def scores_of(head, index):
        return dot_t(queries[low + head, index * ROWS : (index + 1) * ROWS, :], whole(head, 0))

    scores = scores_of(*tiles[0])
    for step, (head, index) in enumerate(tiles):
        ahead = scores_of(*tiles[step + 1]) if step + 1 < len(tiles) else None
        peak = jnp.max(scores, axis=1, keepdims=True)
        weights = jnp.exp2(scores * (SCALE * LOG2E) - peak * (SCALE * LOG2E))
        total = jnp.sum(weights, axis=1, keepdims=True)
        summed = jnp.dot(weights.astype(BF), whole(head, 1), preferred_element_type=F32)
        outs[index][head * ROWS : (head + 1) * ROWS, :] = (summed * (1.0 / total)).astype(BF)
        peaks[index, 0:ROWS, :] = jnp.where(lanes == head, peak, peaks[index, 0:ROWS, :])
        totals[index, 0:ROWS, :] = jnp.where(lanes == head, total, totals[index, 0:ROWS, :])
        scores = ahead
    for index in range(4):
        level = peaks[index] * SCALE + jnp.log(totals[index])
        coarse = level.astype(BF).astype(F32)
        middle = (level - coarse).astype(BF).astype(F32)
        fine = level - coarse - middle
        places = lax.broadcasted_iota(jnp.int32, level.shape, 1)
        parts = jnp.where(places < NQ, coarse, pltpu.roll(middle, NQ, 1))
        turned = jnp.where(places < 2 * NQ, parts, pltpu.roll(fine, 2 * NQ, 1)).T
        outs[index][size : size + 16, :] = turned[0:16, 0:HD].astype(BF)
        outs[index][size + 16 : size + STAT, :] = turned[0:16, HD : 2 * HD].astype(BF)


def attend(group, queries, held, swapped):
    low, count, _, _ = GROUPS[group]
    return call(
        functools.partial(attend_kernel, low, count),
        [shaped((count * ROWS + STAT, HD))] * 4,
        [],
        [queries, held, swapped],
        scratch=[pltpu.VMEM((4, 2 * HD, HD), F32)] * 2,
        flops=4 * count * 4 * ROWS * 8 * KEYS * HD,
        exps=count * 4 * ROWS * 8 * KEYS,
        limit=32,
    )


def combine_kernel(*refs):
    partials = (refs[:4], refs[4:8])
    residuals, attended = refs[8:12], refs[13:17]
    middle_ref, turn_ref = refs[17:]
    turn_ref[...] = jnp.zeros_like(turn_ref)
    squares = jnp.zeros((ROWS, HD), F32)
    for group, (low, count, _, _) in enumerate(GROUPS):
        size = count * ROWS
        levels = []
        for partial in partials[group]:
            turn_ref[0:16, 0:HD] = partial[size : size + 16, :].astype(F32)
            turn_ref[0:16, HD : 2 * HD] = partial[size + 16 : size + STAT, :].astype(F32)
            stat = turn_ref[...].T[0:ROWS, :]
            levels.append(stat + pltpu.roll(stat, HD - NQ, 1) + pltpu.roll(stat, HD - 2 * NQ, 1))
        peak = functools.reduce(jnp.maximum, levels)
        shares = [jnp.exp(level - peak) for level in levels]
        inverse = 1.0 / sum(shares)
        shares = [share * inverse for share in shares]
        for index in range(count):
            head = low + index
            total = sum(
                partial[index * ROWS : (index + 1) * ROWS, :].astype(F32)
                * share[:, index : index + 1]
                for partial, share in zip(partials[group], shares)
            )
            middles = []
            for block in range(4):
                part = total[block * TOK : (block + 1) * TOK].astype(BF)
                attended[block][head] = part
                middle = residuals[block][NQ * min(block, 1) + head].astype(F32) + part.astype(F32)
                middle_ref[head, block] = middle
                middles.append(middle)
            rows = jnp.concatenate(middles, axis=0)
            squares = squares + rows * rows
    sums = jnp.sum(squares, axis=1, keepdims=True)
    lanes = lax.broadcasted_iota(jnp.int32, (TOK, HD), 1)
    packed = jnp.zeros((TOK, HD), F32)
    for block in range(4):
        column = sums[block * TOK : (block + 1) * TOK]
        coarse = column.astype(BF).astype(F32)
        middle = (column - coarse).astype(BF).astype(F32)
        packed = jnp.where(lanes == block, coarse, packed)
        packed = jnp.where(lanes == block + 32, middle, packed)
        packed = jnp.where(lanes == block + 64, column - coarse - middle, packed)
    for block in range(4):
        attended[block][NQ] = packed.astype(BF)


def digits(ids):
    row = lax.broadcasted_iota(jnp.int32, (16, TXT), 0)
    shifts = jnp.where(row == 0, 0, jnp.where(row == 1, 8, 16))
    value = jnp.bitwise_and(lax.shift_right_logical(jnp.broadcast_to(ids, (16, TXT)), shifts), 255)
    return jnp.where(row < 3, value, 0).astype(F32)


def prompt_kernel(
    info_ref, ids_ref, align_ref, gain_ref, text_ref, after_ref, mixed_ref, own_ref, copy_ref, scale_ref, sem
):
    start = pl.multiple_of(info_ref[0] * (NQ * HD), HD)
    copy = pltpu.make_async_copy(text_ref.at[:, :, :, pl.ds(start, NQ * HD)], copy_ref, sem)
    copy.start()
    pairs = lax.broadcasted_iota(jnp.int32, (TXT, TXT), 0) == align_ref[0:1, :]
    chosen = jnp.where(pairs, 1.0, 0.0)
    aligned = jnp.dot(digits(ids_ref[0:1, :]).astype(BF), chosen.astype(BF), preferred_element_type=F32)
    apart = jnp.sum(jnp.abs(aligned - digits(ids_ref[1:2, :])), axis=0, keepdims=True)
    own = jnp.where(apart == 0.0, 0.0, 1.0)
    own_ref[...] = jnp.broadcast_to(own, (8, TXT))
    selection = (chosen * (1.0 - own)).astype(BF)
    scale_ref[...] = jnp.broadcast_to(gain_ref[0:1, pl.ds(start, NQ * HD)].astype(F32), (8, NQ * HD))
    copy.wait()
    mixed_ref[...] = jnp.dot(selection, copy_ref[1, 1], preferred_element_type=F32).astype(BF)


def prompts(info, prompt_ids, word_align, gain, text_kv, after):
    return call(
        prompt_kernel,
        [
            shaped((TXT, NQ * HD)),
            shaped((8, TXT), F32),
            shaped((2, 2, TXT, NQ * HD)),
            shaped((8, NQ * HD), F32),
        ],
        [info],
        [prompt_ids, word_align.reshape(1, TXT), gain.reshape(1, -1)],
        kept=[(text_kv, pltpu.HBM), (after, pl.ANY)],
        scratch=[pltpu.SemaphoreType.DMA],
        flops=2 * TXT * TXT * NQ * HD,
        limit=47,
    )


def pairs_of(info_ref):
    odd = lax.rem(info_ref[1], 2)
    return ((odd, 3 * (1 - odd)), (2 + odd, 1 + odd))


def scores_kernel(info_ref, middle_ref, gain_ref, text_ref, out_ref):
    pairs = pairs_of(info_ref)
    for head in range(NQ):
        columns = slice(head * HD, (head + 1) * HD)
        gain = gain_ref[0:1, columns]
        for side in range(2):
            rows = jnp.concatenate([middle_ref[head, pair[side]] for pair in pairs], axis=0)
            out_ref[side, head] = dot_t((rows * gain).astype(BF), text_ref[0, side, :, columns])


def cross_kernel(info_ref, s0, s1, s2, s3, middle_ref, scores_ref, text_ref, mixed_ref, own_ref, *refs):
    outs, (scale_ref, done_ref) = refs[:4], refs[4:]
    lanes = lax.broadcasted_iota(jnp.int32, (TOK, HD), 1)

    def sums_of(ref):
        packed = ref[NQ].astype(F32)
        return packed + pltpu.roll(packed, HD - 32, 1) + pltpu.roll(packed, HD - 64, 1)

    squares = sums_of(s0)
    for distance, ref in ((1, s1), (2, s2), (3, s3)):
        other = sums_of(ref)
        turned = pltpu.roll(other, HD - distance, 1)
        wrapped = pltpu.roll(other, 4 - distance, 1)
        squares = squares + jnp.where(lanes < 4 - distance, turned, wrapped)
    norm = lax.rsqrt(squares * (1.0 / (4 * NQ * HD)) + 1e-06) * (SCALE * LOG2E)
    for block in range(4):
        scale_ref[block] = jnp.broadcast_to(norm[:, block : block + 1], (TOK, HD))
    pairs = pairs_of(info_ref)
    own = own_ref[0:1, :]
    norms = [
        jnp.concatenate([scale_ref[pair[side]] for pair in pairs], axis=0)[:, 0:1] for side in range(2)
    ]

    def softmax(side, head):
        scores = scores_ref[side, head] * norms[side]
        weights = jnp.exp2(scores - jnp.max(scores, axis=1, keepdims=True))
        return weights * (1.0 / jnp.sum(weights, axis=1, keepdims=True))

    for head in range(NQ):
        columns = slice(head * HD, (head + 1) * HD)
        source = softmax(0, head).astype(BF)
        edited = (softmax(1, head) * own).astype(BF)
        results = (
            jnp.dot(source, text_ref[1, 0, :, columns], preferred_element_type=F32),
            jnp.dot(source, mixed_ref[:, columns], preferred_element_type=F32)
            + jnp.dot(edited, text_ref[1, 1, :, columns], preferred_element_type=F32),
        )
        for side in range(2):
            for index, pair in enumerate(pairs):
                part = results[side][index * TOK : (index + 1) * TOK]
                done_ref[pair[side]] = middle_ref[head, pair[side]] + part
        for block in range(4):
            outs[block][head] = done_ref[block].astype(BF)


def per_device(queries, keys_values, residual_in, cross_gain, text_kv, prompt_ids, word_align):
    plane = 2 * lax.axis_index("yh") + lax.axis_index("yl")
    quarter = 2 * lax.axis_index("yl") + lax.axis_index("yh")
    where = plane.reshape(1).astype(jnp.int32)
    info = jnp.stack([quarter, plane]).astype(jnp.int32)
    piece = (NQ, TOK, HD)

    double = shaped((2 * NQ, TOK, HD))
    first, last = call(split_near_kernel, [double] * 2, [where], [queries[0], residual_in[0]])
    along_x, along_z, over, residual = call(
        split_kernel,
        [
            shaped((WIDE + 2 * NARROW, TOK, HD)),
            shaped((2 * WIDE + NARROW, TOK, HD)),
            shaped((4 * NQ, TOK, HD)),
            shaped(piece),
        ],
        [where],
        [queries[0], residual_in[0], keys_values],
    )

    def gathered(value, axis):
        return [value] + [shift(value, axis, d, 4) for d in (2, 1, 3)]

    first = shift(first, PLANE, 1, 4)
    last = shift(last, PLANE, 3, 4)
    over = shift(over, PLANE, 2, 4)
    units = gathered(along_x, "x") + gathered(along_z, "z")
    along_x, along_z = call(
        pack_kernel,
        [shaped((3 * WIDE + 2 * NARROW, TOK, HD)), shaped((2 * WIDE + 3 * NARROW, TOK, HD))],
        [],
        [first, over, last],
    )
    units = units + gathered(along_x, "x") + gathered(along_z, "z")
    held, rows = call(
        order_kernel, [shaped((2 * NQ, 4 * KEYS, HD)), shaped((NQ, 4 * ROWS, HD))], [], units
    )
    swapped = shift(held, "c", 1, 2)
    partials = []
    for group, (_, _, row_axis, _) in enumerate(GROUPS):
        outs = attend(group, rows, held, swapped)
        partials += [outs[0]] + [shift(outs[i], row_axis, -d, 4) for i, d in ((1, 2), (2, 1), (3, 3))]
    mixed, own, text, gain = prompts(info, prompt_ids, word_align, cross_gain, text_kv, outs[0])
    combined = call(
        combine_kernel,
        [shaped((NQ + 1, TOK, HD))] * 4 + [shaped((NQ, 4, TOK, HD), F32)],
        [],
        [*partials, residual, first, over, last],
        kept=[(own, pl.ANY)],
        scratch=[pltpu.VMEM((HD, 2 * HD), F32)],
    )
    middle = combined[4]

    def home(pieces):
        return [p if d == 0 else shift(p, PLANE, -d, 4) for d, p in enumerate(pieces)]

    def join(pieces):
        return call(join_rows_kernel, [shaped((TOK, 4 * NQ * HD))], [where], pieces)[0]

    attended = home(combined[:4])
    scores = call(
        scores_kernel,
        [shaped((2, NQ, KEYS, TXT), F32)],
        [info],
        [middle, gain, text],
        flops=2 * 2 * KEYS * TXT * NQ * HD,
    )[0]
    results = call(
        cross_kernel,
        [shaped(piece)] * 4,
        [info],
        [*attended, middle, scores, text, mixed, own],
        scratch=[pltpu.VMEM((4, TOK, HD), F32), pltpu.VMEM((4, TOK, HD), F32)],
        flops=2 * 3 * KEYS * TXT * NQ * HD,
        exps=2 * KEYS * NQ * TXT,
        limit=24,
    )
    results = home(results)
    return (join(attended)[None], join(results)[None])


def solution(mesh):
    grid = Mesh(mesh.devices.reshape(4, 2, 4, 2, 2), ("z", "yh", "x", "c", "yl"))
    seq = ("z", "yh", "x", "c")
    in_specs = (
        P("yl", seq, None),
        P(None, seq, "yl"),
        P("yl", seq, None),
        P(),
        P(),
        P(),
        P(),
    )
    out_specs = (P("yl", seq, None), P("yl", seq, None))
    return jax.shard_map(per_device, mesh=grid, in_specs=in_specs, out_specs=out_specs, check_vma=False)
```
